512 devices in a mesh: scen: 32 (over z, y_lo, core), col: 16 (over x, y_hi).
Axes of the slice: x: 4, y: 8 (y_hi: 4, y_lo: 2; y = y_hi * 2 + y_lo), z: 8, core: 2. Of those that a mesh axis runs over, the one named last changes fastest.
Arguments:
- inverse_factor: bfloat16 [512, 512, 512], P(('scen', 'col')), as said below
- true_orders: int32 [512], P(('scen', 'col')), may hold values from 64 to 512, as said below
- slab_border: bfloat16 [512, 256, 512], P(('scen', 'col')), may hold values from -0.25 to 0.25
- slab_columns: int32 [512, 256], P('scen'), may hold values from 0 to 511
- panel_border: bfloat16 [16, 512, 48, 512], P('col', 'scen'), may hold values from -6 to 6
- panel_rows: int32 [16, 512, 48], P('col', 'scen'), may hold values from 0 to 479
- barrier_diag: float32 [512], replicated, may hold values from 20 to 400
Outputs:
- diag_factor: float32 [512, 512], P('col')
- panel_factor: float32 [7680, 512], P(('scen', 'col'))
The draws below stay inside these ranges and needn't reach their ends.
Inputs may be any that keep to these rules, and one draw needn't show every extreme that they name: `inverse_factor`: symmetric; its leading block of each scenario's true order is positive definite. `true_orders`: scenario 0 has the full padded order.
All inputs are finite; a program needn't handle non-finite values.
Results may differ from the reference program's by a relative error of at most 0.0003.
The reference program's roundings to bfloat16 on the way (of `masked` and `transformed`) count: a program that leaves them out, or rounds other values in their place, can miss the bound.
Values may be sent and summed in bfloat16 or wider, within the bound.
A program may use at most 64 MiB of HBM per device.

```python
import math
import jax
import jax.numpy as jnp
from jax import lax

P_SIZE = 512
DIAG = 512
CBJ = 256
CBP = 48
SCEN = 512
ROWS_PANEL = 480
ROWS_DEV = 15
N_SCEN = 32
N_COL = 16


def draw_inverse_factor(key, part):

    def draw_single(position):
        folded = jax.random.fold_in(key, position)
        first_key, second_key = jax.random.split(folded)
        noise = jax.random.normal(first_key, (P_SIZE, P_SIZE), jnp.float32)
        symmetric = (noise + noise.T) * (0.4 / math.sqrt(2.0 * P_SIZE))
        leading = jax.random.uniform(second_key, (P_SIZE,), jnp.float32, 1.5, 2.5)
        return (symmetric + jnp.diag(leading)).astype(jnp.bfloat16)
    return lax.map(draw_single, jnp.arange(SCEN, dtype=jnp.int32))


def draw_true_orders(key, part):
    values = jax.random.randint(key, (SCEN,), P_SIZE // 8, P_SIZE + 1, dtype=jnp.int32)
    values = values.at[0].set(P_SIZE)
    return values.at[1].set(P_SIZE // 8)


def place_ends(entries, rng, low, high):
    dims = entries.shape
    place = [jax.random.randint(jax.random.fold_in(rng, axis), (), 0, dims[axis]) for axis in range(len(dims))]
    entries = entries.at[tuple(place)].set(low)
    longest = dims.index(max(dims))
    place[longest] = (place[longest] + 1) % dims[longest]
    return entries.at[tuple(place)].set(high)


def steps_of(own_key, extent, cuts, low, high):
    def one(dim, shards_of):
        draws = jax.random.uniform(jax.random.fold_in(jax.random.fold_in(own_key, 6), dim), (shards_of,), jnp.float32, low / len(cuts), high / len(cuts))
        return jnp.repeat(jnp.exp(draws), extent[dim] // shards_of).reshape((-1,) + (1,) * (len(extent) - dim - 1))

    factor_of = one(*cuts[0])
    for cut in cuts[1:]:
        factor_of = factor_of * one(*cut)
    return factor_of


def normal_values(stream_key, shape, width, limit, cuts=(), kind=jnp.bfloat16):
    array = jax.random.normal(stream_key, shape, jnp.float32) * width
    if len(cuts) > 0:
        array = steps_of(stream_key, shape, cuts, -0.22, 0.18) * array
    return jnp.clip(array, min=-limit, max=limit).astype(kind)


def setup_inputs(seed: int = 0) -> dict:
    streams_of = jax.random.split(jax.random.key(seed), 8)
    return {
        "inverse_factor": draw_inverse_factor(jax.random.fold_in(streams_of[7], 71), 0),
        "true_orders": draw_true_orders(jax.random.fold_in(streams_of[7], 71), 0),
        "slab_border": normal_values(streams_of[2], (SCEN, CBJ, P_SIZE), P_SIZE ** -0.5, 0.25, ((0, 512),)),
        "slab_columns": place_ends(jax.random.randint(streams_of[3], (SCEN, CBJ), 0, DIAG), jax.random.fold_in(streams_of[3], 1), 0, DIAG - 1).astype(jnp.int32),
        "panel_border": normal_values(streams_of[4], (N_COL, SCEN, CBP, P_SIZE), 1.0, 6.0, ((0, 16), (1, 32))),
        "panel_rows": place_ends(jax.random.randint(streams_of[5], (N_COL, SCEN, CBP), 0, ROWS_PANEL), jax.random.fold_in(streams_of[5], 1), 0, ROWS_PANEL - 1).astype(jnp.int32),
        "barrier_diag": jnp.clip(jnp.exp(jax.random.uniform(streams_of[6], (DIAG,), jnp.float32, math.log(20.0), math.log(400.0))), 20.0, 400.0),
    }


def reference(inverse_factor, true_orders, slab_border, slab_columns, panel_border, panel_rows, barrier_diag):
    positions = jnp.arange(P_SIZE, dtype=jnp.int32)

    def transform(operands):
        factor, order_value, border = operands
        inside = positions < order_value
        masked = jnp.where(inside[:, None] & inside[None, :], factor, jnp.zeros((), jnp.bfloat16))
        return jnp.dot(border.astype(jnp.float32), masked.astype(jnp.float32), preferred_element_type=jnp.float32).astype(jnp.bfloat16)
    transformed = lax.map(transform, (inverse_factor, true_orders, slab_border))

    def diag_step(running, operands):
        border, moved_rows, columns = operands
        coupling = jnp.dot(border.astype(jnp.float32), moved_rows.T.astype(jnp.float32), preferred_element_type=jnp.float32)
        return (running.at[columns[:, None], columns[None, :]].add(coupling), None)
    schur_diag, _ = lax.scan(diag_step, jnp.diag(barrier_diag), (slab_border, transformed, slab_columns))

    def panel_total(operands):
        border_part, rows_part = operands

        def panel_step(running, inner):
            border_values, moved_rows, row_index, columns = inner
            coupling = jnp.dot(border_values.astype(jnp.float32), moved_rows.T.astype(jnp.float32), preferred_element_type=jnp.float32)
            return (running.at[row_index[:, None], columns[None, :]].add(coupling), None)
        zero_panel = jnp.zeros((ROWS_PANEL, DIAG), jnp.float32)
        result, _ = lax.scan(panel_step, zero_panel, (border_part, transformed, rows_part, slab_columns))
        return result
    panels = lax.map(panel_total, (panel_border, panel_rows))
    slab_rows = panels.reshape(N_COL, N_SCEN, ROWS_DEV, DIAG).transpose(1, 0, 2, 3).reshape(N_COL * ROWS_PANEL, DIAG)
    symmetric = 0.5 * (schur_diag + schur_diag.T)
    diag_factor = jnp.linalg.cholesky(symmetric)
    panel_factor = lax.linalg.triangular_solve(diag_factor, slab_rows, left_side=False, lower=True, transpose_a=True)
    return (diag_factor, panel_factor)
```

```python
import functools

import jax
import jax.numpy as jnp
from jax import lax
from jax.experimental import pallas as pl
from jax.experimental.pallas import tpu as pltpu
from jax.sharding import PartitionSpec as P

HIGHEST = lax.Precision.HIGHEST
MESH = pl.DeviceIdType.MESH
F32 = jnp.float32
BF16 = jnp.bfloat16
DIAG = 512
NB = DIAG // 128
BLOCKS = [(r, j) for r in range(NB) for j in range(r, NB)]
TILES = 16 * len(BLOCKS)


def split(value, parts):
    out = []
    for _ in range(parts - 1):
        piece = value.astype(BF16)
        out.append(piece)
        value = value - piece.astype(F32)
    return out + [value.astype(BF16)]


def dot(a, b, ca, cb, precision=None):
    return lax.dot_general(
        a, b, (((ca,), (cb,)), ((), ())), precision=precision, preferred_element_type=F32
    )


def one_hot(targets, height):
    width = targets.shape[1]
    place = lax.broadcasted_iota(jnp.int32, (height, width), 0)
    return jnp.where(place == targets, 1.0, 0.0).astype(BF16)


class Wire:
    def __init__(self, send_sem, recv_sem):
        self.send_sem, self.recv_sem, self.used, self.sends = send_sem, recv_sem, 0, []

    def start(self, src, dst, scen, col):
        k = self.used
        self.used += 1
        copy = pltpu.make_async_remote_copy(
            src_ref=src,
            dst_ref=dst,
            send_sem=self.send_sem.at[k],
            recv_sem=self.recv_sem.at[k],
            device_id=(scen, col),
            device_id_type=MESH,
        )
        copy.start()
        self.sends.append(copy)
        return copy

    def drain(self):
        for copy in self.sends:
            copy.wait_send()


def exchange_kernel(
    n_x, n_y, n_zy,
    order_ref, inv_ref, border_ref, columns_ref, panel_ref, rows_ref,
    diag_ref, slab_ref,
    pb, tr, coup, coup_in, packed, c_buf, half, z_buf, y_own, y_buf, x_own, x_buf, full,
    maps, row_map, wide, total, pc_buf, p_half, pz_buf,
    send_sem, recv_sem, local_sem,
):
    scen, col = lax.axis_index("scen"), lax.axis_index("col")
    core, zy = scen % 2, scen // 2
    x, y = col // n_y, col % n_y
    sibling = scen + 1 - 2 * core
    n_tiles = TILES // 2
    chunk = n_tiles // n_zy
    p_rows = total.shape[0] // 2
    p_chunk = p_rows // n_zy
    wire = Wire(send_sem, recv_sem)

    barrier = pltpu.get_barrier_semaphore()
    zy_peers = [((zy + d) % n_zy) for d in range(1, n_zy)]
    y_peers = [((y + d) % n_y) for d in range(1, n_y)]
    x_peers = [((x + d) % n_x) for d in range(1, n_x)]
    greet = [(sibling, col)]
    greet += [(p * 2 + core, col) for p in zy_peers]
    greet += [(scen, x * n_y + p) for p in y_peers]
    greet += [(scen, p * n_y + y) for p in x_peers]
    for device in greet:
        pl.semaphore_signal(barrier, inc=1, device_id=device, device_id_type=MESH)
    pl.semaphore_wait(barrier, len(greet))

    pb_copies = [
        wire.start(panel_ref.at[0, pl.ds(p * n_y, n_y)], pb.at[:, x], scen, p * n_y + y)
        for p in x_peers
    ]
    own_pb = pltpu.make_async_copy(panel_ref.at[0, pl.ds(x * n_y, n_y)], pb.at[:, x], local_sem.at[0])
    own_pb.start()

    order = order_ref[0]
    p_size = inv_ref.shape[1]
    border = border_ref[0]
    lanes = lax.broadcasted_iota(jnp.int32, border.shape, 1)
    inside = lanes < order
    cut = jnp.where(inside, border.astype(F32), 0.0).astype(BF16)
    moved = dot(cut, inv_ref[0], 1, 0)
    moved = jnp.where(inside, moved, 0.0).astype(BF16)
    tr[y] = moved
    tr_copies = [wire.start(tr.at[y], tr.at[y], scen, x * n_y + p) for p in y_peers]

    terms = 0.5 * (dot(border, moved, 1, 1) + dot(moved, border, 1, 1))
    own_map = one_hot(columns_ref[pl.ds(col, 1), :], DIAG)
    spread = sum(dot(own_map, piece, 1, 0) for piece in split(terms, 3))
    pieces = split(spread, 3)
    base = 0
    for r in range(NB):
        rows = slice(128 * r, 128 * r + 128)
        strip = sum(dot(piece[rows], own_map[128 * r :], 1, 1) for piece in pieces)
        for j in range(r, NB):
            block = strip[:, 128 * (j - r) : 128 * (j - r + 1)]
            packed[base : base + 16] = block.reshape(16, 8, 128)
            base += 16

    c_copy = wire.start(packed.at[pl.ds((1 - core) * n_tiles, n_tiles)], c_buf, sibling, col)
    flat = rows_ref[...]
    rows_dev = 15
    owner = (flat * 4370) >> 16
    slot = (owner % 2) * p_rows + (owner // 2) * p_chunk + (flat - owner * rows_dev)
    row_map[...] = one_hot(slot, 2 * p_rows)
    c_copy.wait_recv()
    half[...] = packed[pl.ds(core * n_tiles, n_tiles)] + c_buf[...]

    z_copies = [
        wire.start(half.at[pl.ds(p * chunk, chunk)], z_buf.at[k], p * 2 + core, col)
        for k, p in enumerate(zy_peers)
    ]

    def build_map(i, carry):
        maps[i] = one_hot(columns_ref[pl.ds(i, 1), :], DIAG)
        return carry

    lax.fori_loop(0, maps.shape[0], build_map, 0)
    for copy in z_copies:
        copy.wait_recv()
    y_own[...] = half[pl.ds(zy * chunk, chunk)] + jnp.sum(z_buf[...], axis=0)
    y_copies = [
        wire.start(y_own, y_buf.at[k], scen, x * n_y + p) for k, p in enumerate(y_peers)
    ]
    for copy in y_copies:
        copy.wait_recv()
    x_own[...] = y_own[...] + jnp.sum(y_buf[...], axis=0)
    x_copies = [
        wire.start(x_own, x_buf.at[k], scen, p * n_y + y) for k, p in enumerate(x_peers)
    ]
    for copy in x_copies:
        copy.wait_recv()
    mine = pl.ds((core * n_zy + zy) * chunk, chunk)
    full[mine] = x_own[...] + jnp.sum(x_buf[...], axis=0)
    g_copies = [wire.start(full.at[mine], full.at[mine], p * 2 + core, col) for p in zy_peers]

    own_pb.wait()
    for copy in pb_copies:
        copy.wait_recv()
    for copy in tr_copies:
        copy.wait_recv()

    def couple(i, carry):
        stacked = pb[i].reshape(n_x * pb.shape[2], p_size)
        coup[i] = dot(stacked, tr[i], 1, 1).reshape(coup.shape[1:])
        return carry

    lax.fori_loop(0, n_y, couple, 0)
    own_coup = pltpu.make_async_copy(coup.at[:, x], coup_in.at[pl.ds(x * n_y, n_y)], local_sem.at[1])
    own_coup.start()
    q_copies = [
        wire.start(coup.at[:, p], coup_in.at[pl.ds(x * n_y, n_y)], scen, p * n_y + y)
        for p in x_peers
    ]

    for copy in g_copies:
        copy.wait_recv()
    side = pl.ds(core * n_tiles, n_tiles)
    h_copy = wire.start(full.at[side], full.at[side], sibling, col)
    own_coup.wait()
    for copy in q_copies:
        copy.wait_recv()

    n_b = coup.shape[2]

    def widen(i, carry):
        high, low = split(coup_in[i], 2)
        both = dot(jnp.concatenate([high, low], axis=0), maps[i], 1, 1)
        wide[pl.ds(i * n_b, n_b), :] = both[:n_b] + both[n_b:]
        return carry

    lax.fori_loop(0, maps.shape[0], widen, 0)
    high, low = split(wide[...], 2)
    total[...] = dot(row_map[...], high, 1, 0) + dot(row_map[...], low, 1, 0)
    pc_copy = wire.start(total.at[pl.ds((1 - core) * p_rows, p_rows)], pc_buf, sibling, col)
    pc_copy.wait_recv()
    p_half[...] = total[pl.ds(core * p_rows, p_rows)] + pc_buf[...]
    pz_copies = [
        wire.start(p_half.at[pl.ds(p * p_chunk, p_chunk)], pz_buf.at[k], p * 2 + core, col)
        for k, p in enumerate(zy_peers)
    ]
    h_copy.wait_recv()
    diag_ref[...] = full[...]
    for copy in pz_copies:
        copy.wait_recv()
    slab_ref[...] = p_half[pl.ds(zy * p_chunk, p_chunk)] + jnp.sum(pz_buf[...], axis=0)
    wire.drain()


def exchange(n_x, n_y, n_zy, order, inverse_factor, border, columns, panel_border, flat_rows):
    n_scen = columns.shape[0]
    cbj, p_size = border.shape[1:]
    cbp = panel_border.shape[2]
    chunk = TILES // 2 // n_zy
    p_rows = 16 * n_zy
    n_copies = 2 + 3 * (n_zy - 1) + 2 * (n_y - 1) + 3 * (n_x - 1) + 1
    tile = (8, 128)
    vmem = pl.BlockSpec(memory_space=pltpu.VMEM)
    return pl.pallas_call(
        functools.partial(exchange_kernel, n_x, n_y, n_zy),
        name="exchange",
        out_shape=(
            jax.ShapeDtypeStruct((TILES,) + tile, F32),
            jax.ShapeDtypeStruct((16, DIAG), F32),
        ),
        in_specs=[pl.BlockSpec(memory_space=pltpu.SMEM)] + [vmem] * 5,
        out_specs=[vmem] * 2,
        scratch_shapes=[
            pltpu.VMEM((n_y, n_x, cbp, p_size), BF16),
            pltpu.VMEM((n_y, cbj, p_size), BF16),
            pltpu.VMEM((n_y, n_x, cbp, cbj), F32),
            pltpu.VMEM((n_scen, cbp, cbj), F32),
            pltpu.VMEM((TILES,) + tile, F32),
            pltpu.VMEM((TILES // 2,) + tile, F32),
            pltpu.VMEM((TILES // 2,) + tile, F32),
            pltpu.VMEM((n_zy - 1, chunk) + tile, F32),
            pltpu.VMEM((chunk,) + tile, F32),
            pltpu.VMEM((n_y - 1, chunk) + tile, F32),
            pltpu.VMEM((chunk,) + tile, F32),
            pltpu.VMEM((n_x - 1, chunk) + tile, F32),
            pltpu.VMEM((TILES,) + tile, F32),
            pltpu.VMEM((n_scen, DIAG, cbj), BF16),
            pltpu.VMEM((2 * p_rows, n_scen * cbp), BF16),
            pltpu.VMEM((n_scen * cbp, DIAG), F32),
            pltpu.VMEM((2 * p_rows, DIAG), F32),
            pltpu.VMEM((p_rows, DIAG), F32),
            pltpu.VMEM((p_rows, DIAG), F32),
            pltpu.VMEM((n_zy - 1, 16, DIAG), F32),
            pltpu.SemaphoreType.DMA((n_copies,)),
            pltpu.SemaphoreType.DMA((n_copies,)),
            pltpu.SemaphoreType.DMA((2,)),
        ],
        compiler_params=pltpu.CompilerParams(collective_id=0, has_side_effects=True),
    )(order, inverse_factor, border, columns, panel_border, flat_rows)


def factor_block(block):
    groups = 16
    tile = (8, 128)
    lane = lax.broadcasted_iota(jnp.int32, tile, 1)
    sub = lax.broadcasted_iota(jnp.int32, tile, 0)
    left = [block[8 * q : 8 * q + 8, :] for q in range(groups)]
    right = [jnp.where(lane == sub + 8 * q, 1.0, 0.0).astype(F32) for q in range(groups)]
    upper, inverse = [], []

    def spread(row):
        return jnp.broadcast_to(row, tile)

    for p in range(groups):
        column = {
            q: [jnp.broadcast_to(left[q][:, 8 * p + m : 8 * p + m + 1], tile) for m in range(8)]
            for q in range(p, groups)
        }
        pivot = column[p]
        row_l, row_r = left[p], right[p]
        out_l, out_r = jnp.zeros(tile, F32), jnp.zeros(tile, F32)
        for t in range(4):
            m, k = 2 * t, 2 * t + 1
            a, b, c = spread(pivot[m][m : m + 1]), spread(pivot[k][m : m + 1]), spread(pivot[k][k : k + 1])
            det = a * c - b * b
            over = 1.0 / det
            ia, ib, ic = c * over, -(b * over), a * over
            for n in range(k + 1, 8):
                e, f = spread(pivot[n][m : m + 1]), spread(pivot[n][k : k + 1])
                g, h = ia * e + ib * f, ib * e + ic * f
                for q in range(p, groups):
                    column[q][n] = column[q][n] - (column[q][m] * g + column[q][k] * h)
            lm, lk = spread(row_l[m : m + 1]), spread(row_l[k : k + 1])
            rm, rk = spread(row_r[m : m + 1]), spread(row_r[k : k + 1])
            l0, l1 = ia * lm + ib * lk, ib * lm + ic * lk
            r0, r1 = ia * rm + ib * rk, ib * rm + ic * rk
            if k < 7:
                cm = jnp.where(sub > k, pivot[m], 0.0)
                ck = jnp.where(sub > k, pivot[k], 0.0)
                row_l = row_l - (cm * l0 + ck * l1)
                row_r = row_r - (cm * r0 + ck * r1)
            s0 = lax.rsqrt(a)
            s1 = lax.rsqrt(det) * (a * s0)
            ratio = b * s0 * s0
            out_l = jnp.where(sub == m, lm * s0, jnp.where(sub == k, (lk - ratio * lm) * s1, out_l))
            out_r = jnp.where(sub == m, rm * s0, jnp.where(sub == k, (rk - ratio * rm) * s1, out_r))
            for q in range(p + 1, groups):
                left[q] = left[q] - (column[q][m] * l0 + column[q][k] * l1)
                right[q] = right[q] - (column[q][m] * r0 + column[q][k] * r1)
        upper.append(jnp.where(lane >= sub + 8 * p, out_l, 0.0))
        inverse.append(out_r)
    return jnp.concatenate(upper, 0), jnp.concatenate(inverse, 0)


def factor_kernel(packed_ref, barrier_ref, slab_ref, col_ref, diag_ref, panel_ref, work, upper):
    eye = lax.broadcasted_iota(jnp.int32, (128, 128), 0) == lax.broadcasted_iota(jnp.int32, (128, 128), 1)
    for k, (r, j) in enumerate(BLOCKS):
        block = packed_ref[16 * k : 16 * k + 16].reshape(128, 128)
        if r == j:
            block = block + jnp.where(eye, barrier_ref[:, 128 * r : 128 * r + 128], 0.0)
        work[128 * r : 128 * r + 128, 128 * j : 128 * j + 128] = block
    upper[...] = jnp.zeros(upper.shape, F32)
    rows = slab_ref[...]
    solved = []
    for b in range(NB):
        o = 128 * b
        u, inv = factor_block(work[o : o + 128, o : o + 128])
        upper[o : o + 128, o : o + 128] = u
        done = dot(rows[:, :128], inv, 1, 1, HIGHEST)
        solved.append(done)
        if b < NB - 1:
            beside = dot(inv, work[o : o + 128, o + 128 :], 1, 0, HIGHEST)
            upper[o : o + 128, o + 128 :] = beside
            for j in range(b + 1, NB):
                lead = beside[:, 128 * (j - b - 1) : 128 * (j - b)]
                tail = beside[:, 128 * (j - b - 1) :]
                work[128 * j : 128 * j + 128, 128 * j :] -= dot(lead, tail, 0, 0, HIGHEST)
            rows = rows[:, 128:] - dot(done, beside, 1, 0, HIGHEST)
    n_out = diag_ref.shape[0]
    first = col_ref[0] * n_out
    pick = lax.broadcasted_iota(jnp.int32, (n_out, DIAG), 1) == first + lax.broadcasted_iota(
        jnp.int32, (n_out, DIAG), 0
    )
    diag_ref[...] = dot(jnp.where(pick, 1.0, 0.0), upper[...], 1, 1, HIGHEST)
    panel_ref[...] = jnp.concatenate(solved, axis=1)[: panel_ref.shape[0]]


def factor(packed, barrier_diag, slab, col, diag_rows, panel_rows):
    vmem = pl.BlockSpec(memory_space=pltpu.VMEM)
    return pl.pallas_call(
        factor_kernel,
        name="factor",
        out_shape=(
            jax.ShapeDtypeStruct((diag_rows, DIAG), F32),
            jax.ShapeDtypeStruct((panel_rows, DIAG), F32),
        ),
        in_specs=[vmem] * 3 + [pl.BlockSpec(memory_space=pltpu.SMEM)],
        out_specs=[vmem] * 2,
        scratch_shapes=[pltpu.VMEM((DIAG, DIAG), F32), pltpu.VMEM((DIAG, DIAG), F32)],
    )(packed, barrier_diag.reshape(1, DIAG), slab, col)


def shards(
    inverse_factor, true_orders, slab_border, slab_columns, panel_border, panel_rows, barrier_diag
):
    n_scen, n_col = lax.axis_size("scen"), lax.axis_size("col")
    n_y = {16: 4, 4: 2}[n_col]
    packed, slab = exchange(
        n_col // n_y,
        n_y,
        n_scen // 2,
        true_orders,
        inverse_factor,
        slab_border,
        slab_columns,
        panel_border,
        panel_rows.reshape(1, -1),
    )
    col = lax.axis_index("col").astype(jnp.int32).reshape(1)
    return factor(packed, barrier_diag, slab, col, DIAG // n_col, 15)


def solution(mesh):
    in_specs = (
        P(("scen", "col"), None, None),
        P(("scen", "col")),
        P(("scen", "col"), None, None),
        P("scen", None),
        P("col", "scen", None, None),
        P("col", "scen", None),
        P(),
    )
    out_specs = (P("col", None), P(("scen", "col"), None))
    return jax.shard_map(shards, mesh=mesh, in_specs=in_specs, out_specs=out_specs, check_vma=False)
```

```python
import functools

import jax
import jax.numpy as jnp
from jax import lax
from jax.experimental import pallas as pl
from jax.experimental.pallas import tpu as pltpu
from jax.sharding import PartitionSpec as P

HIGHEST = lax.Precision.HIGHEST
MESH = pl.DeviceIdType.MESH
F32 = jnp.float32
BF16 = jnp.bfloat16
DIAG = 512
NB = DIAG // 128
BLOCKS = [(r, j) for r in range(NB) for j in range(r, NB)]
TILES = 16 * len(BLOCKS)


def split(value, parts):
    out = []
    for _ in range(parts - 1):
        piece = value.astype(BF16)
        out.append(piece)
        value = value - piece.astype(F32)
    return out + [value.astype(BF16)]


def dot(a, b, ca, cb, precision=None):
    return lax.dot_general(
        a, b, (((ca,), (cb,)), ((), ())), precision=precision, preferred_element_type=F32
    )


def one_hot(targets, height):
    width = targets.shape[1]
    place = lax.broadcasted_iota(jnp.int32, (height, width), 0)
    return jnp.where(place == targets, 1.0, 0.0).astype(BF16)


class Wire:
    def __init__(self, send_sem, recv_sem):
        self.send_sem, self.recv_sem, self.used, self.sends = send_sem, recv_sem, 0, []

    def start(self, src, dst, scen, col):
        k = self.used
        self.used += 1
        copy = pltpu.make_async_remote_copy(
            src_ref=src,
            dst_ref=dst,
            send_sem=self.send_sem.at[k],
            recv_sem=self.recv_sem.at[k],
            device_id=(scen, col),
            device_id_type=MESH,
        )
        copy.start()
        self.sends.append(copy)
        return copy

    def drain(self):
        for copy in self.sends:
            copy.wait_send()


def factor_block(block):
    groups = 16
    tile = (8, 128)
    lane = lax.broadcasted_iota(jnp.int32, tile, 1)
    sub = lax.broadcasted_iota(jnp.int32, tile, 0)
    whole = (groups,) + tile
    left = block.reshape(whole)
    place = 8 * lax.broadcasted_iota(jnp.int32, whole, 0) + lax.broadcasted_iota(jnp.int32, whole, 1)
    right = jnp.where(lax.broadcasted_iota(jnp.int32, whole, 2) == place, 1.0, 0.0)
    upper, inverse = [], []

    def spread(row):
        return jnp.broadcast_to(row, tile)

    for p in range(groups):
        shape = (groups - p,) + tile
        column = [jnp.broadcast_to(left[:, :, 8 * p + m : 8 * p + m + 1], shape) for m in range(8)]
        row_l, row_r = left[0], right[0]
        left, right = left[1:], right[1:]
        out_l, out_r = jnp.zeros(tile, F32), jnp.zeros(tile, F32)
        for t in range(4):
            m, k = 2 * t, 2 * t + 1
            col_m, col_k = column[m], column[k]
            a, b, c = spread(col_m[0, m : m + 1]), spread(col_k[0, m : m + 1]), spread(col_k[0, k : k + 1])
            det = a * c - b * b
            over = 1.0 / det
            ia, ib, ic = c * over, -(b * over), a * over
            for n in range(k + 1, 8):
                e, f = spread(column[n][0, m : m + 1]), spread(column[n][0, k : k + 1])
                g, h = ia * e + ib * f, ib * e + ic * f
                column[n] = column[n] - (col_m * g + col_k * h)
            lm, lk = spread(row_l[m : m + 1]), spread(row_l[k : k + 1])
            rm, rk = spread(row_r[m : m + 1]), spread(row_r[k : k + 1])
            l0, l1 = ia * lm + ib * lk, ib * lm + ic * lk
            r0, r1 = ia * rm + ib * rk, ib * rm + ic * rk
            if k < 7:
                cm = jnp.where(sub > k, col_m[0], 0.0)
                ck = jnp.where(sub > k, col_k[0], 0.0)
                row_l = row_l - (cm * l0 + ck * l1)
                row_r = row_r - (cm * r0 + ck * r1)
            s0 = lax.rsqrt(a)
            s1 = lax.rsqrt(det) * (a * s0)
            ratio = b * s0 * s0
            out_l = jnp.where(sub == m, lm * s0, jnp.where(sub == k, (lk - ratio * lm) * s1, out_l))
            out_r = jnp.where(sub == m, rm * s0, jnp.where(sub == k, (rk - ratio * rm) * s1, out_r))
            if p < groups - 1:
                left = left - (col_m[1:] * l0 + col_k[1:] * l1)
                right = right - (col_m[1:] * r0 + col_k[1:] * r1)
        upper.append(jnp.where(lane >= sub + 8 * p, out_l, 0.0))
        inverse.append(out_r)
    return jnp.concatenate(upper, 0), jnp.concatenate(inverse, 0)


def kernel(
    n_x, n_y, n_z,
    order_ref, columns_ref, rows_ref, bar_ref, inv_ref, border_ref, panel_ref,
    diag_ref, slab_ref,
    factor_in, border_in, pb, tr, coup, coup_in, packed, c_buf, half, z_buf, z_sum, l_buf, y_own, y_buf,
    x_own, x_buf, full, maps, flat_buf, row_map, wide, total, pc_buf, p_half, pz_buf,
    work, upper, inverse,
    send_sem, recv_sem, local_sem,
):
    scen, col = lax.axis_index("scen"), lax.axis_index("col")
    core, l, z = scen % 2, (scen // 2) % 2, scen // 4
    x, y = col // n_y, col % n_y
    zy, n_zy = scen // 2, 2 * n_z
    sibling = scen + 1 - 2 * core
    beside_y = scen + 2 - 4 * l
    n_tiles = TILES // 2
    z_chunk = n_tiles // n_z
    chunk = z_chunk // 2
    p_rows = total.shape[0] // 2
    p_chunk = p_rows // n_zy
    p_size = inv_ref.shape[1]
    wire = Wire(send_sem, recv_sem)

    with jax.named_scope("barrier"):
        loads = [
            pltpu.make_async_copy(inv_ref.at[0], factor_in, local_sem.at[0]),
            pltpu.make_async_copy(border_ref.at[0], border_in, local_sem.at[1]),
            pltpu.make_async_copy(panel_ref.at[0, pl.ds(x * n_y, n_y)], pb.at[:, x], local_sem.at[2]),
        ]
        for load in loads:
            load.start()
        barrier = pltpu.get_barrier_semaphore()
        zy_peers = [((zy + d) % n_zy) * 2 + core for d in range(1, n_zy)]
        z_peers = [(z + d) % n_z for d in range(1, n_z)]
        y_peers = [(y + d) % n_y for d in range(1, n_y)]
        x_peers = [(x + d) % n_x for d in range(1, n_x)]
        greet = [(sibling, col)] + [(p, col) for p in zy_peers]
        greet += [(scen, x * n_y + p) for p in y_peers] + [(scen, p * n_y + y) for p in x_peers]
        for device in greet:
            pl.semaphore_signal(barrier, inc=1, device_id=device, device_id_type=MESH)
        pl.semaphore_wait(barrier, len(greet))

    def z_device(p):
        return p * 4 + l * 2 + core

    with jax.named_scope("transform"):
        pb_copies = [
            wire.start(panel_ref.at[0, pl.ds(p * n_y, n_y)], pb.at[:, x], scen, p * n_y + y) for p in x_peers
        ]
        loads[0].wait()
        loads[1].wait()
        order = order_ref[0]
        border = border_in[...]
        inside = lax.broadcasted_iota(jnp.int32, border.shape, 1) < order
        cut = jnp.where(inside, border.astype(F32), 0.0).astype(BF16)
        moved = dot(cut, factor_in[...], 1, 0)
        moved = jnp.where(inside, moved, 0.0).astype(BF16)
        tr[y] = moved
        near = [(y + 1) % n_y] + ([(y + n_y - 1) % n_y] if n_y > 2 else [])
        tr_copies = [wire.start(tr.at[y], tr.at[y], scen, x * n_y + p) for p in near]

    with jax.named_scope("diag"):
        terms = 0.5 * (dot(border, moved, 1, 1) + dot(moved, border, 1, 1))
        own_map = one_hot(columns_ref[pl.ds(col, 1), :], DIAG)
        spread = sum(dot(own_map, piece, 1, 0) for piece in split(terms, 3))
        pieces = split(spread, 3)
        base = 0
        for r in range(NB):
            rows = slice(128 * r, 128 * r + 128)
            strip = sum(dot(piece[rows], own_map[128 * r :], 1, 1) for piece in pieces)
            for j in range(r, NB):
                block = strip[:, 128 * (j - r) : 128 * (j - r + 1)]
                packed[base : base + 16] = block.reshape(16, 8, 128)
                base += 16

    with jax.named_scope("cores"):
        c_copy = wire.start(packed.at[pl.ds((1 - core) * n_tiles, n_tiles)], c_buf, sibling, col)
        n_scen, n_b = rows_ref.shape[1:]
        for i in range(n_scen):
            flat_buf[:, n_b * i : n_b * i + n_b] = rows_ref[0, i : i + 1, :]
        flat = flat_buf[...]
        owner = (flat * 4370) >> 16
        slot = (owner % 2) * p_rows + (owner // 2) * p_chunk + (flat - owner * 15)
        row_map[...] = one_hot(slot, 2 * p_rows)
        c_copy.wait_recv()
        half[...] = packed[pl.ds(core * n_tiles, n_tiles)] + c_buf[...]

    with jax.named_scope("z_sum"):
        z_copies = [
            wire.start(half.at[pl.ds(p * z_chunk, z_chunk)], z_buf.at[k], z_device(p), col)
            for k, p in enumerate(z_peers)
        ]

        def build_map(i, carry):
            maps[i] = one_hot(columns_ref[pl.ds(i, 1), :], DIAG)
            return carry

        lax.fori_loop(0, n_scen, build_map, 0)
    with jax.named_scope("z_wait"):
        for copy in z_copies:
            copy.wait_recv()
        z_sum[...] = half[pl.ds(z * z_chunk, z_chunk)]
        if n_z > 1:
            z_sum[...] += jnp.sum(z_buf[...], axis=0)
    with jax.named_scope("l_wait"):
        l_copy = wire.start(z_sum.at[pl.ds((1 - l) * chunk, chunk)], l_buf, beside_y, col)
        l_copy.wait_recv()
        y_own[...] = z_sum[pl.ds(l * chunk, chunk)] + l_buf[...]
        y_copies = [wire.start(y_own, y_buf.at[k], scen, x * n_y + p) for k, p in enumerate(y_peers)]

    with jax.named_scope("tr_wait"):
        for copy in tr_copies:
            copy.wait_recv()
        far_copies = []
        if n_y == 4:
            h = tr.shape[1] // 2
            up, down = (y + 1) % n_y, (y + n_y - 1) % n_y
            first, second = tr.at[down, pl.ds(0, h)], tr.at[up, pl.ds(h, h)]
            far_copies = [
                wire.start(first, first, scen, x * n_y + up),
                wire.start(second, second, scen, x * n_y + down),
            ]
        loads[2].wait()
        for copy in pb_copies:
            copy.wait_recv()

    def couple(i):
        stacked = pb[i].reshape(n_x * n_b, p_size)
        coup[i] = dot(stacked, tr[i], 1, 1).reshape(coup.shape[1:])
        coup_in[x * n_y + i] = coup[i, x]

    def give(i):
        return [wire.start(coup.at[i, p], coup_in.at[x * n_y + i], scen, p * n_y + y) for p in x_peers]

    with jax.named_scope("couple"):
        for i in [y] + near:
            couple(i)
    with jax.named_scope("y_wait"):
        for copy in y_copies:
            copy.wait_recv()
        x_own[...] = y_own[...] + jnp.sum(y_buf[...], axis=0)
        x_copies = [wire.start(x_own, x_buf.at[k], scen, p * n_y + y) for k, p in enumerate(x_peers)]
        q_copies = [copy for i in [y] + near for copy in give(i)]
    with jax.named_scope("x_wait"):
        for copy in x_copies:
            copy.wait_recv()
        mine = pl.ds(((core * n_z + z) * 2 + l) * chunk, chunk)
        full[mine] = x_own[...] + jnp.sum(x_buf[...], axis=0) if n_x > 1 else x_own[...]
    with jax.named_scope("l_gather"):
        lg_copy = wire.start(full.at[mine], full.at[mine], beside_y, col)
        lg_copy.wait_recv()
    with jax.named_scope("z_gather"):
        pair = pl.ds((core * n_z + z) * z_chunk, z_chunk)
        zg_copies = [wire.start(full.at[pair], full.at[pair], z_device(p), col) for p in z_peers]
        for copy in far_copies:
            copy.wait_recv()
        if n_y == 4:
            far = (y + 2) % n_y
            couple(far)
            q_copies += give(far)
    with jax.named_scope("q_wait"):
        for copy in q_copies:
            copy.wait_recv()

    with jax.named_scope("widen"):

        def widen(i, carry):
            high, low = split(coup_in[i], 2)
            both = dot(jnp.concatenate([high, low], axis=0), maps[i], 1, 1)
            wide[pl.ds(i * n_b, n_b), :] = both[:n_b] + both[n_b:]
            return carry

        lax.fori_loop(0, n_scen, widen, 0)
        high, low = split(wide[...], 2)
        total[...] = dot(row_map[...], high, 1, 0) + dot(row_map[...], low, 1, 0)
        pc_copy = wire.start(total.at[pl.ds((1 - core) * p_rows, p_rows)], pc_buf, sibling, col)

    with jax.named_scope("zg_wait"):
        for copy in zg_copies:
            copy.wait_recv()
        side = pl.ds(core * n_tiles, n_tiles)
        h_copy = wire.start(full.at[side], full.at[side], sibling, col)
    with jax.named_scope("pc_wait"):
        pc_copy.wait_recv()
        p_half[...] = total[pl.ds(core * p_rows, p_rows)] + pc_buf[...]
        pz_copies = [
            wire.start(p_half.at[pl.ds(((zy + d) % n_zy) * p_chunk, p_chunk)], pz_buf.at[d - 1], zy_peers[d - 1], col)
            for d in range(1, n_zy)
        ]
        upper[...] = jnp.zeros(upper.shape, F32)
    with jax.named_scope("h_wait"):
        h_copy.wait_recv()

    with jax.named_scope("load"):
        rr = lax.broadcasted_iota(jnp.int32, (128, 128), 0)
        cc = lax.broadcasted_iota(jnp.int32, (128, 128), 1)
        for k, (r, j) in enumerate(BLOCKS):
            block = full[16 * k : 16 * k + 16].reshape(128, 128)
            if r == j:
                block = block + jnp.where(rr == cc, bar_ref[:, 128 * r : 128 * r + 128], 0.0)
            work[128 * r : 128 * r + 128, 128 * j : 128 * j + 128] = block

    def step(b, carry):
        o = pl.multiple_of(b * 128, 128)
        with jax.named_scope("block"):
            u, inv = factor_block(work[pl.ds(o, 128), pl.ds(o, 128)])
            upper[pl.ds(o, 128), pl.ds(o, 128)] = u
            inverse[pl.ds(o, 128), :] = inv
        for k in range(NB - 1):

            @pl.when(b == k)
            def _():
                with jax.named_scope("trail"):
                    s = 128 * k
                    beside = dot(inv, work[s : s + 128, s + 128 :], 1, 0, HIGHEST)
                    upper[s : s + 128, s + 128 :] = beside
                    for j in range(k + 1, NB):
                        lead = beside[:, 128 * (j - k - 1) : 128 * (j - k)]
                        tail = beside[:, 128 * (j - k - 1) :]
                        work[128 * j : 128 * j + 128, 128 * j :] -= dot(lead, tail, 0, 0, HIGHEST)

        return carry

    lax.fori_loop(0, NB, step, 0)

    with jax.named_scope("pick"):
        n_out = diag_ref.shape[0]
        pick = lax.broadcasted_iota(jnp.int32, (n_out, DIAG), 1) == col * n_out + lax.broadcasted_iota(
            jnp.int32, (n_out, DIAG), 0
        )
        diag_ref[...] = dot(jnp.where(pick, 1.0, 0.0), upper[...], 1, 1, HIGHEST)
    with jax.named_scope("pz_wait"):
        for copy in pz_copies:
            copy.wait_recv()
    with jax.named_scope("solve"):
        rows = p_half[pl.ds(zy * p_chunk, p_chunk)] + jnp.sum(pz_buf[...], axis=0)
        solved = []
        for b in range(NB):
            done = dot(rows[:, :128], inverse[128 * b : 128 * b + 128, :], 1, 1, HIGHEST)
            solved.append(done)
            if b < NB - 1:
                rows = rows[:, 128:] - dot(done, upper[128 * b : 128 * b + 128, 128 * b + 128 :], 1, 0, HIGHEST)
        slab_ref[...] = jnp.concatenate(solved, axis=1)[: slab_ref.shape[0]]
    wire.drain()


def shards(
    inverse_factor, true_orders, slab_border, slab_columns, panel_border, panel_rows, barrier_diag
):
    n_col = lax.axis_size("col")
    n_z = lax.axis_size("scen") // 4
    n_y = min(n_col, 4) if n_col != 4 else 2
    n_x = n_col // n_y
    n_scen = slab_columns.shape[0]
    cbj, p_size = slab_border.shape[1:]
    cbp = panel_border.shape[2]
    z_chunk = TILES // 2 // n_z
    p_rows = 32 * n_z
    n_copies = 64
    tile = (8, 128)
    vmem = pl.BlockSpec(memory_space=pltpu.VMEM)
    anywhere = pl.BlockSpec(memory_space=pl.ANY)
    scratch = [
        ((p_size, p_size), BF16),
        ((cbj, p_size), BF16),
        ((n_y, n_x, cbp, p_size), BF16),
        ((n_y, cbj, p_size), BF16),
        ((n_y, n_x, cbp, cbj), F32),
        ((n_scen, cbp, cbj), F32),
        ((TILES,) + tile, F32),
        ((TILES // 2,) + tile, F32),
        ((TILES // 2,) + tile, F32),
        ((max(n_z - 1, 1), z_chunk) + tile, F32),
        ((z_chunk,) + tile, F32),
        ((z_chunk // 2,) + tile, F32),
        ((z_chunk // 2,) + tile, F32),
        ((n_y - 1, z_chunk // 2) + tile, F32),
        ((z_chunk // 2,) + tile, F32),
        ((max(n_x - 1, 1), z_chunk // 2) + tile, F32),
        ((TILES,) + tile, F32),
        ((n_scen, DIAG, cbj), BF16),
        ((1, n_scen * cbp), jnp.int32),
        ((2 * p_rows, n_scen * cbp), BF16),
        ((n_scen * cbp, DIAG), F32),
        ((2 * p_rows, DIAG), F32),
        ((p_rows, DIAG), F32),
        ((p_rows, DIAG), F32),
        ((2 * n_z - 1, 16, DIAG), F32),
        ((DIAG, DIAG), F32),
        ((DIAG, DIAG), F32),
        ((DIAG, 128), F32),
    ]
    return pl.pallas_call(
        functools.partial(kernel, n_x, n_y, n_z),
        name="slab",
        out_shape=(
            jax.ShapeDtypeStruct((DIAG // n_col, DIAG), F32),
            jax.ShapeDtypeStruct((15, DIAG), F32),
        ),
        in_specs=[pl.BlockSpec(memory_space=pltpu.SMEM)] + [vmem] * 3 + [anywhere] * 3,
        out_specs=[vmem] * 2,
        scratch_shapes=[pltpu.VMEM(*one) for one in scratch]
        + [
            pltpu.SemaphoreType.DMA((n_copies,)),
            pltpu.SemaphoreType.DMA((n_copies,)),
            pltpu.SemaphoreType.DMA((3,)),
        ],
        compiler_params=pltpu.CompilerParams(collective_id=0, has_side_effects=True),
    )(
        true_orders,
        slab_columns,
        panel_rows,
        barrier_diag.reshape(1, DIAG),
        inverse_factor,
        slab_border,
        panel_border,
    )


def solution(mesh):
    in_specs = (
        P(("scen", "col"), None, None),
        P(("scen", "col")),
        P(("scen", "col"), None, None),
        P("scen", None),
        P("col", "scen", None, None),
        P("col", "scen", None),
        P(),
    )
    out_specs = (P("col", None), P(("scen", "col"), None))
    return jax.shard_map(shards, mesh=mesh, in_specs=in_specs, out_specs=out_specs, check_vma=False)
```

```python
import functools

import jax
import jax.numpy as jnp
from jax import lax
from jax.experimental import pallas as pl
from jax.experimental.pallas import tpu as pltpu
from jax.sharding import PartitionSpec as P

HIGHEST = lax.Precision.HIGHEST
MESH = pl.DeviceIdType.MESH
F32 = jnp.float32
BF16 = jnp.bfloat16
DIAG = 512
NB = DIAG // 128
BLOCKS = [(r, j) for r in range(NB) for j in range(r, NB)]
TILES = 16 * len(BLOCKS)


def split(value, parts):
    out = []
    for _ in range(parts - 1):
        piece = value.astype(BF16)
        out.append(piece)
        value = value - piece.astype(F32)
    return out + [value.astype(BF16)]


def dot(a, b, ca, cb, precision=None):
    return lax.dot_general(
        a, b, (((ca,), (cb,)), ((), ())), precision=precision, preferred_element_type=F32
    )


def one_hot(targets, height):
    width = targets.shape[1]
    place = lax.broadcasted_iota(jnp.int32, (height, width), 0)
    return jnp.where(place == targets, 1.0, 0.0).astype(BF16)


class Wire:
    def __init__(self, send_sem, recv_sem):
        self.send_sem, self.recv_sem, self.used, self.sends = send_sem, recv_sem, 0, []

    def start(self, src, dst, scen, col):
        k = self.used
        self.used += 1
        copy = pltpu.make_async_remote_copy(
            src_ref=src,
            dst_ref=dst,
            send_sem=self.send_sem.at[k],
            recv_sem=self.recv_sem.at[k],
            device_id=(scen, col),
            device_id_type=MESH,
        )
        copy.start()
        self.sends.append(copy)
        return copy

    def drain(self, keep=0):
        done = len(self.sends) - keep
        for copy in self.sends[:done]:
            copy.wait_send()
        self.sends = self.sends[done:]


def factor_block(block):
    groups = 16
    tile = (8, 128)
    lane = lax.broadcasted_iota(jnp.int32, tile, 1)
    sub = lax.broadcasted_iota(jnp.int32, tile, 0)
    whole = (groups,) + tile
    left = block.reshape(whole)
    place = 8 * lax.broadcasted_iota(jnp.int32, whole, 0) + lax.broadcasted_iota(jnp.int32, whole, 1)
    right = jnp.where(lax.broadcasted_iota(jnp.int32, whole, 2) == place, 1.0, 0.0)
    upper, inverse = [], []

    def spread(row):
        return jnp.broadcast_to(row, tile)

    for p in range(groups):
        shape = (groups - p,) + tile
        column = [jnp.broadcast_to(left[:, :, 8 * p + m : 8 * p + m + 1], shape) for m in range(8)]
        row_l, row_r = left[0], right[0]
        left, right = left[1:], right[1:]
        out_l, out_r = jnp.zeros(tile, F32), jnp.zeros(tile, F32)
        for t in range(4):
            m, k = 2 * t, 2 * t + 1
            col_m, col_k = column[m], column[k]
            a, b, c = spread(col_m[0, m : m + 1]), spread(col_k[0, m : m + 1]), spread(col_k[0, k : k + 1])
            det = a * c - b * b
            over = 1.0 / det
            ia, ib, ic = c * over, -(b * over), a * over
            for n in range(k + 1, 8):
                e, f = spread(column[n][0, m : m + 1]), spread(column[n][0, k : k + 1])
                g, h = ia * e + ib * f, ib * e + ic * f
                column[n] = column[n] - (col_m * g + col_k * h)
            lm, lk = spread(row_l[m : m + 1]), spread(row_l[k : k + 1])
            rm, rk = spread(row_r[m : m + 1]), spread(row_r[k : k + 1])
            l0, l1 = ia * lm + ib * lk, ib * lm + ic * lk
            r0, r1 = ia * rm + ib * rk, ib * rm + ic * rk
            if k < 7:
                cm = jnp.where(sub > k, col_m[0], 0.0)
                ck = jnp.where(sub > k, col_k[0], 0.0)
                row_l = row_l - (cm * l0 + ck * l1)
                row_r = row_r - (cm * r0 + ck * r1)
            s0 = lax.rsqrt(a)
            s1 = lax.rsqrt(det) * (a * s0)
            ratio = b * s0 * s0
            out_l = jnp.where(sub == m, lm * s0, jnp.where(sub == k, (lk - ratio * lm) * s1, out_l))
            out_r = jnp.where(sub == m, rm * s0, jnp.where(sub == k, (rk - ratio * rm) * s1, out_r))
            if p < groups - 1:
                left = left - (col_m[1:] * l0 + col_k[1:] * l1)
                right = right - (col_m[1:] * r0 + col_k[1:] * r1)
        upper.append(jnp.where(lane >= sub + 8 * p, out_l, 0.0))
        inverse.append(out_r)
    return jnp.concatenate(upper, 0), jnp.concatenate(inverse, 0)


def kernel(
    n_x, n_y, n_z,
    order_ref, columns_ref, rows_ref, bar_ref, inv_ref, border_ref, panel_ref,
    diag_ref, slab_ref,
    order_in, columns_in, rows_in, bar_in, factor_in, border_in,
    pb, tr, coup, coup_in, packed, c_buf, half, z_buf, z_sum, l_buf, y_own, y_buf,
    x_own, x_buf, full, maps, flat_buf, row_map, wide, total, pc_buf, p_half, pz_buf,
    work, upper, inverse, turned,
    send_sem, recv_sem, local_sem,
):
    scen, col = lax.axis_index("scen"), lax.axis_index("col")
    core, l, z = scen % 2, (scen // 2) % 2, scen // 4
    x, y = col // n_y, col % n_y
    zy, n_zy = scen // 2, 2 * n_z
    sibling = scen + 1 - 2 * core
    beside_y = scen + 2 - 4 * l
    first, rest = 16 // n_z, 24 // n_z
    parts = (pl.ds(0, first), pl.ds(first, rest))
    p_rows = total.shape[0] // 2
    p_chunk = p_rows // n_zy
    p_size = inv_ref.shape[1]
    n_scen, n_b = rows_ref.shape[1:]
    wire = Wire(send_sem, recv_sem)

    with jax.named_scope("barrier"):
        loads = [
            pltpu.make_async_copy(src, dst, local_sem.at[k])
            for k, (src, dst) in enumerate(
                (
                    (inv_ref.at[0], factor_in),
                    (border_ref.at[0], border_in),
                    (order_ref, order_in),
                    (columns_ref, columns_in),
                    (rows_ref, rows_in),
                    (bar_ref, bar_in),
                    (panel_ref.at[0, pl.ds(x * n_y, n_y)], pb.at[:, x]),
                )
            )
        ]
        for load in loads:
            load.start()
        barrier = pltpu.get_barrier_semaphore()
        zy_peers = [((zy + d) % n_zy) * 2 + core for d in range(1, n_zy)]
        z_peers = [(z + d) % n_z for d in range(1, n_z)]
        y_peers = [(y + d) % n_y for d in range(1, n_y)]
        x_peers = [(x + d) % n_x for d in range(1, n_x)]
        greet = [(sibling, col)] + [(p, col) for p in zy_peers]
        greet += [(scen, x * n_y + p) for p in y_peers] + [(scen, p * n_y + y) for p in x_peers]
        for device in greet:
            pl.semaphore_signal(barrier, inc=1, device_id=device, device_id_type=MESH)

    def arrive(copies):
        for copy in copies:
            copy.wait_recv()

    with jax.named_scope("transform"):
        for load in loads[:4]:
            load.wait()
        order = order_in[0]
        border = border_in[...]
        inside = lax.broadcasted_iota(jnp.int32, border.shape, 1) < order
        cut = jnp.where(inside, border.astype(F32), 0.0).astype(BF16)
        moved = dot(cut, factor_in[...], 1, 0)
        moved = jnp.where(inside, moved, 0.0).astype(BF16)
        tr[y] = moved
        pl.semaphore_wait(barrier, len(greet))
        near = [(y + 1) % n_y] + ([(y + n_y - 1) % n_y] if n_y > 2 else [])
        tr_copies = [wire.start(tr.at[y], tr.at[y], scen, x * n_y + p) for p in near]
        pb_copies = [
            wire.start(panel_ref.at[0, pl.ds(p * n_y, n_y)], pb.at[:, x], scen, p * n_y + y) for p in x_peers
        ]

    with jax.named_scope("diag"):
        terms = 0.5 * (dot(border, moved, 1, 1) + dot(moved, border, 1, 1))
        own_map = one_hot(columns_in[pl.ds(col, 1), :], DIAG)
        spread = sum(dot(own_map, piece, 1, 0) for piece in split(terms, 3))
        pieces = split(spread, 3)
        c_copies = []
        for r in range(NB):
            rows = slice(128 * r, 128 * r + 128)
            strip = sum(dot(piece[rows], own_map[128 * r :], 1, 1) for piece in pieces)
            for j in range(r, NB):
                block = strip[:, 128 * (j - r) : 128 * (j - r + 1)]
                for t in range(16):
                    packed[where_tile(n_z, r, j, t)] = block[8 * t : 8 * t + 8]
            if r == 0:
                c_copies.append(
                    wire.start(packed.at[1 - core, :, :, parts[0]], c_buf.at[:, :, parts[0]], sibling, col)
                )
        c_copies.append(wire.start(packed.at[1 - core, :, :, parts[1]], c_buf.at[:, :, parts[1]], sibling, col))

    def add_cores(k):
        c_copies[k].wait_recv()
        half[:, :, parts[k]] = packed[core, :, :, parts[k]] + c_buf[:, :, parts[k]]
        return [
            wire.start(half.at[p, :, parts[k]], z_buf.at[i, :, parts[k]], p * 4 + l * 2 + core, col)
            for i, p in enumerate(z_peers)
        ]

    def add_z(k, copies):
        arrive(copies)
        mine = half[z, :, parts[k]]
        z_sum[:, parts[k]] = mine + jnp.sum(z_buf[:, :, parts[k]], axis=0) if n_z > 1 else mine
        return [wire.start(z_sum.at[1 - l, parts[k]], l_buf.at[parts[k]], beside_y, col)]

    def add_l(k, copies):
        arrive(copies)
        y_own[parts[k]] = z_sum[l, parts[k]] + l_buf[parts[k]]
        return [
            wire.start(y_own.at[parts[k]], y_buf.at[i, parts[k]], scen, x * n_y + p) for i, p in enumerate(y_peers)
        ]

    def add_y(k, copies):
        arrive(copies)
        x_own[parts[k]] = y_own[parts[k]] + jnp.sum(y_buf[:, parts[k]], axis=0)
        return [
            wire.start(x_own.at[parts[k]], x_buf.at[i, parts[k]], scen, p * n_y + y) for i, p in enumerate(x_peers)
        ]

    def add_x(k, copies):
        arrive(copies)
        full[core, z, l, parts[k]] = x_own[parts[k]] + jnp.sum(x_buf[:, parts[k]], axis=0)
        here = full.at[core, z, l, parts[k]]
        return [wire.start(here, here, beside_y, col)]

    def gather_z(k, copies):
        arrive(copies)
        here = full.at[core, z, :, parts[k]]
        return [wire.start(here, here, p * 4 + l * 2 + core, col) for p in z_peers]

    def gather_cores(k, copies):
        arrive(copies)
        here = full.at[core, :, :, parts[k]]
        return [wire.start(here, here, sibling, col)]

    def couple(i):
        stacked = pb[i].reshape(n_x * n_b, p_size)
        coup[i] = dot(stacked, tr[i], 1, 1).reshape(coup.shape[1:])
        coup_in[x * n_y + i] = coup[i, x]

    def give(i):
        return [wire.start(coup.at[i, p], coup_in.at[x * n_y + i], scen, p * n_y + y) for p in x_peers]

    def widen(i):
        high, low = split(coup_in[i], 2)
        both = dot(jnp.concatenate([high, low], axis=0), maps[i], 1, 1)
        at = i * n_b
        wide[pl.ds(pl.multiple_of(at, 16), n_b), :] = both[:n_b] + both[n_b:]

    with jax.named_scope("cores0"):
        s0 = add_cores(0)
    with jax.named_scope("cores1"):
        s1 = add_cores(1)
    with jax.named_scope("maps"):
        loads[4].wait()
        loads[5].wait()
        for i in range(n_scen):
            flat_buf[:, n_b * i : n_b * i + n_b] = rows_in[0, i : i + 1, :]
        flat = flat_buf[...]
        owner = (flat * 4370) >> 16
        slot = (owner % 2) * p_rows + (owner // 2) * p_chunk + (flat - owner * 15)
        row_map[...] = one_hot(slot, 2 * p_rows)

        def build_map(i, carry):
            maps[i] = one_hot(columns_in[pl.ds(i, 1), :], DIAG)
            return carry

        lax.fori_loop(0, n_scen, build_map, 0)
        upper[...] = jnp.zeros(upper.shape, F32)
    with jax.named_scope("z0"):
        s0 = add_z(0, s0)
    with jax.named_scope("l0"):
        s0 = add_l(0, s0)
    with jax.named_scope("z1"):
        s1 = add_z(1, s1)
    with jax.named_scope("tr_wait"):
        arrive(tr_copies)
        far_copies = []
        if n_y == 4:
            h = tr.shape[1] // 2
            up, down = (y + 1) % n_y, (y + n_y - 1) % n_y
            low_half, high_half = tr.at[down, pl.ds(0, h)], tr.at[up, pl.ds(h, h)]
            far_copies = [
                wire.start(low_half, low_half, scen, x * n_y + up),
                wire.start(high_half, high_half, scen, x * n_y + down),
            ]
        loads[6].wait()
        arrive(pb_copies)
    with jax.named_scope("couple"):
        for i in [y] + near:
            couple(i)
    with jax.named_scope("y0"):
        s0 = add_y(0, s0)
        q_near = [copy for i in [y] + near for copy in give(i)]
    with jax.named_scope("l1"):
        s1 = add_l(1, s1)
    with jax.named_scope("x0"):
        s0 = add_x(0, s0)
    with jax.named_scope("lg0"):
        s0 = gather_z(0, s0)
    with jax.named_scope("y1"):
        s1 = add_y(1, s1)
    with jax.named_scope("far"):
        q_far = []
        if n_y == 4:
            arrive(far_copies)
            far = (y + 2) % n_y
            couple(far)
            q_far = give(far)
    with jax.named_scope("q_near"):
        arrive(q_near)
    with jax.named_scope("widen_near"):
        for i in [y] + near:
            for k in range(n_x):
                widen(k * n_y + i)
    with jax.named_scope("x1"):
        s1 = add_x(1, s1)
    with jax.named_scope("zg0"):
        s0 = gather_cores(0, s0)
    with jax.named_scope("lg1"):
        s1 = gather_z(1, s1)
    with jax.named_scope("q_far"):
        arrive(q_far)
    with jax.named_scope("widen_far"):
        if n_y == 4:
            for k in range(n_x):
                widen(k * n_y + far)
    with jax.named_scope("total"):
        high, low = split(wide[...], 2)
        total[...] = dot(row_map[...], high, 1, 0) + dot(row_map[...], low, 1, 0)
        pc_copy = wire.start(total.at[pl.ds((1 - core) * p_rows, p_rows)], pc_buf, sibling, col)
    with jax.named_scope("drain0"):
        wire.drain(2 * n_z + 2)
    with jax.named_scope("hg0"):
        arrive(s0)

    rr = lax.broadcasted_iota(jnp.int32, (128, 128), 0)
    cc = lax.broadcasted_iota(jnp.int32, (128, 128), 1)

    def load_row(r):
        for j in range(r, NB):
            block = jnp.concatenate([full[where_tile(n_z, r, j, t)] for t in range(16)], axis=0)
            if r == j:
                block = block + jnp.where(rr == cc, bar_in[:, 128 * r : 128 * r + 128], 0.0)
            work[128 * r : 128 * r + 128, 128 * j : 128 * j + 128] = block

    def block_step(o):
        with jax.named_scope("block"):
            u, inv = factor_block(work[pl.ds(o, 128), pl.ds(o, 128)])
            upper[pl.ds(o, 128), pl.ds(o, 128)] = u
            inverse[pl.ds(o, 128), :] = inv
        return inv

    def trail(k, inv):
        with jax.named_scope("trail"):
            s = 128 * k
            beside = dot(inv, work[s : s + 128, s + 128 :], 1, 0, HIGHEST)
            upper[s : s + 128, s + 128 :] = beside
            for j in range(k + 1, NB):
                lead = beside[:, 128 * (j - k - 1) : 128 * (j - k)]
                tail = beside[:, 128 * (j - k - 1) :]
                work[128 * j : 128 * j + 128, 128 * j :] -= dot(lead, tail, 0, 0, HIGHEST)

    load_row(0)
    inv = block_step(0)
    with jax.named_scope("zg1"):
        s1 = gather_cores(1, s1)
    with jax.named_scope("hg1"):
        arrive(s1)
        for r in range(1, NB):
            load_row(r)
    trail(0, inv)
    with jax.named_scope("pc_wait"):
        pc_copy.wait_recv()
        p_half[...] = total[pl.ds(core * p_rows, p_rows)] + pc_buf[...]
        pz_copies = [
            wire.start(p_half.at[pl.ds(((zy + d) % n_zy) * p_chunk, p_chunk)], pz_buf.at[d - 1], zy_peers[d - 1], col)
            for d in range(1, n_zy)
        ]

    def step(b, carry):
        inv = block_step(pl.multiple_of(b * 128, 128))
        for k in range(1, NB - 1):

            @pl.when(b == k)
            def _():
                trail(k, inv)

        return carry

    lax.fori_loop(1, NB, step, 0)

    with jax.named_scope("pick"):
        n_out = diag_ref.shape[0]
        start = col * n_out
        turned[...] = jnp.transpose(upper[:, pl.ds(pl.multiple_of(start // 128 * 128, 128), 128)])
        diag_ref[...] = turned[pl.ds(pl.multiple_of(start % 128, 8), n_out), :]
    with jax.named_scope("pz_wait"):
        arrive(pz_copies)
    with jax.named_scope("solve"):
        rows = p_half[pl.ds(zy * p_chunk, p_chunk)] + jnp.sum(pz_buf[...], axis=0)
        solved = []
        for b in range(NB):
            done = dot(rows[:, :128], inverse[128 * b : 128 * b + 128, :], 1, 1, HIGHEST)
            solved.append(done)
            if b < NB - 1:
                rows = rows[:, 128:] - dot(done, upper[128 * b : 128 * b + 128, 128 * b + 128 :], 1, 0, HIGHEST)
        slab_ref[...] = jnp.concatenate(solved, axis=1)[: slab_ref.shape[0]]
    with jax.named_scope("drain1"):
        wire.drain()


def out_kernel(diag_ref, slab_ref, diag_out, slab_out):
    diag_out[...] = diag_ref[...]
    slab_out[...] = slab_ref[...]


def where_tile(n_z, r, j, t):
    first, rest = 16 // n_z, 24 // n_z
    at = 16 * BLOCKS.index((r, j)) + t
    if r == 0:
        chunk, e = at // first, at % first
    else:
        at -= 16 * NB
        chunk, e = at // rest, first + at % rest
    return chunk // (2 * n_z), chunk // 2 % n_z, chunk % 2, e


def shards(
    inverse_factor, true_orders, slab_border, slab_columns, panel_border, panel_rows, barrier_diag
):
    n_col = lax.axis_size("col")
    n_z = lax.axis_size("scen") // 4
    n_y = min(n_col, 4) if n_col != 4 else 2
    n_x = n_col // n_y
    n_scen = slab_columns.shape[0]
    cbj, p_size = slab_border.shape[1:]
    cbp = panel_border.shape[2]
    chunk = TILES // 4 // n_z
    p_rows = 32 * n_z
    n_copies = 96
    tile = (8, 128)
    vmem = pl.BlockSpec(memory_space=pltpu.VMEM)
    anywhere = pl.BlockSpec(memory_space=pl.ANY)
    scratch = [
        pltpu.SMEM((1,), jnp.int32),
        pltpu.VMEM(slab_columns.shape, jnp.int32),
        pltpu.VMEM(panel_rows.shape, jnp.int32),
        pltpu.VMEM((1, DIAG), F32),
        pltpu.VMEM((p_size, p_size), BF16),
        pltpu.VMEM((cbj, p_size), BF16),
        pltpu.VMEM((n_y, n_x, cbp, p_size), BF16),
        pltpu.VMEM((n_y, cbj, p_size), BF16),
        pltpu.VMEM((n_y, n_x, cbp, cbj), F32),
        pltpu.VMEM((n_scen, cbp, cbj), F32),
        pltpu.VMEM((2, n_z, 2, chunk) + tile, F32),
        pltpu.VMEM((n_z, 2, chunk) + tile, F32),
        pltpu.VMEM((n_z, 2, chunk) + tile, F32),
        pltpu.VMEM((max(n_z - 1, 1), 2, chunk) + tile, F32),
        pltpu.VMEM((2, chunk) + tile, F32),
        pltpu.VMEM((chunk,) + tile, F32),
        pltpu.VMEM((chunk,) + tile, F32),
        pltpu.VMEM((n_y - 1, chunk) + tile, F32),
        pltpu.VMEM((chunk,) + tile, F32),
        pltpu.VMEM((max(n_x - 1, 1), chunk) + tile, F32),
        pltpu.VMEM((2, n_z, 2, chunk) + tile, F32),
        pltpu.VMEM((n_scen, DIAG, cbj), BF16),
        pltpu.VMEM((1, n_scen * cbp), jnp.int32),
        pltpu.VMEM((2 * p_rows, n_scen * cbp), BF16),
        pltpu.VMEM((n_scen * cbp, DIAG), F32),
        pltpu.VMEM((2 * p_rows, DIAG), F32),
        pltpu.VMEM((p_rows, DIAG), F32),
        pltpu.VMEM((p_rows, DIAG), F32),
        pltpu.VMEM((2 * n_z - 1, 16, DIAG), F32),
        pltpu.VMEM((DIAG, DIAG), F32),
        pltpu.VMEM((DIAG, DIAG), F32),
        pltpu.VMEM((DIAG, 128), F32),
        pltpu.VMEM((128, DIAG), F32),
        pltpu.SemaphoreType.DMA((n_copies,)),
        pltpu.SemaphoreType.DMA((n_copies,)),
        pltpu.SemaphoreType.DMA((7,)),
    ]
    factored = pl.pallas_call(
        functools.partial(kernel, n_x, n_y, n_z),
        name="slab",
        out_shape=tuple(
            pltpu.VMEM(shape, F32) for shape in ((DIAG // n_col, DIAG), (15, DIAG))
        ),
        in_specs=[anywhere] * 7,
        out_specs=[vmem] * 2,
        scratch_shapes=scratch,
        compiler_params=pltpu.CompilerParams(collective_id=0, has_side_effects=True),
    )(
        true_orders,
        slab_columns,
        panel_rows,
        barrier_diag.reshape(1, DIAG),
        inverse_factor,
        slab_border,
        panel_border,
    )
    return pl.pallas_call(
        out_kernel,
        name="out",
        out_shape=(
            jax.ShapeDtypeStruct((DIAG // n_col, DIAG), F32),
            jax.ShapeDtypeStruct((15, DIAG), F32),
        ),
        in_specs=[vmem] * 2,
        out_specs=[vmem] * 2,
    )(*(pltpu.with_memory_space_constraint(one, pltpu.VMEM) for one in factored))


def solution(mesh):
    in_specs = (
        P(("scen", "col"), None, None),
        P(("scen", "col")),
        P(("scen", "col"), None, None),
        P("scen", None),
        P("col", "scen", None, None),
        P("col", "scen", None),
        P(),
    )
    out_specs = (P("col", None), P(("scen", "col"), None))
    return jax.shard_map(shards, mesh=mesh, in_specs=in_specs, out_specs=out_specs, check_vma=False)
```

```python
import functools

import jax
import jax.numpy as jnp
from jax import lax
from jax.experimental import pallas as pl
from jax.experimental.pallas import tpu as pltpu
from jax.sharding import PartitionSpec as P

HIGHEST = lax.Precision.HIGHEST
MESH = pl.DeviceIdType.MESH
F32 = jnp.float32
BF16 = jnp.bfloat16
DIAG = 512
NB = DIAG // 128
BLOCKS = [(r, j) for r in range(NB) for j in range(r, NB)]
TILES = 16 * len(BLOCKS)


def split(value, parts):
    out = []
    for _ in range(parts - 1):
        piece = value.astype(BF16)
        out.append(piece)
        value = value - piece.astype(F32)
    return out + [value.astype(BF16)]


def dot(a, b, ca, cb, precision=None):
    return lax.dot_general(
        a, b, (((ca,), (cb,)), ((), ())), precision=precision, preferred_element_type=F32
    )


def one_hot(targets, height):
    width = targets.shape[1]
    place = lax.broadcasted_iota(jnp.int32, (height, width), 0)
    return jnp.where(place == targets, 1.0, 0.0).astype(BF16)


class Wire:
    def __init__(self, send_sem, recv_sem):
        self.send_sem, self.recv_sem, self.used, self.sends = send_sem, recv_sem, 0, []

    def start(self, group, view=None):
        sems = self.send_sem.at[self.used], self.recv_sem.at[self.used]
        self.used += 1
        for src, dst, scen, col in group:
            pltpu.make_async_remote_copy(src, dst, *sems, (scen, col), MESH).start()
        if group:
            view = group[0][1] if view is None else view
            whole = pltpu.make_async_remote_copy(view, view, *sems, group[0][2:], MESH)
            self.sends.append(whole)
            return [whole]
        return []

    def drain(self, keep=0):
        done = len(self.sends) - keep
        for copy in self.sends[:done]:
            copy.wait_send()
        self.sends = self.sends[done:]


def tree(terms):
    while len(terms) > 1:
        terms = [sum(terms[i : i + 2]) for i in range(0, len(terms), 2)]
    return terms[0]


def factor_block(block, zero):
    groups = 16
    tile = (8, 128)
    lane = lax.broadcasted_iota(jnp.int32, tile, 1)
    sub = lax.broadcasted_iota(jnp.int32, tile, 0)
    whole = (groups,) + tile
    left = block.reshape(whole)
    place = 8 * lax.broadcasted_iota(jnp.int32, whole, 0) + lax.broadcasted_iota(jnp.int32, whole, 1)
    right = jnp.where(lax.broadcasted_iota(jnp.int32, whole, 2) == place, 1.0, 0.0)
    upper, inverse = [], []

    def spread(value, m):
        return jnp.broadcast_to(value[m : m + 1], tile)

    for p in range(groups):
        rows = [left[0], right[0]]
        column = [jnp.broadcast_to(rows[0][:, 8 * p + m : 8 * p + m + 1], tile) + zero for m in range(8)]
        out = [jnp.zeros(tile, F32)] * 2
        below, solved = {}, [[None] * 8, [None] * 8]
        for m in range(0, 8, 2):
            k = m + 1
            col_m, col_k = column[m], column[k]
            a, b, c = spread(col_m, m), spread(col_k, m), spread(col_k, k)
            det = a * c - b * b
            over = 1.0 / det
            ia, ib, ic = c * over, -(b * over), a * over
            for n in range(k + 1, 8):
                e, f = spread(column[n], m), spread(column[n], k)
                g, h = ia * e + ib * f, ib * e + ic * f
                below[m, n], below[k, n] = g, h
                column[n] = column[n] - (col_m * g + col_k * h)
            s0 = lax.rsqrt(a)
            s1 = lax.rsqrt(det) * (a * s0)
            ratio = b * s0 * s0
            under = sub > k
            for w in range(2):
                first, second = spread(rows[w], m), spread(rows[w], k)
                y0, y1 = ia * first + ib * second, ib * first + ic * second
                solved[w][m], solved[w][k] = y0, y1
                if k < 7:
                    rows[w] = rows[w] - jnp.where(under, col_m * y0 + col_k * y1, 0.0)
                out[w] = jnp.where(
                    sub == m, first * s0, jnp.where(sub == k, (second - ratio * first) * s1, out[w])
                )
        upper.append(jnp.where(lane >= sub + 8 * p, out[0], 0.0))
        inverse.append(out[1])
        if p == groups - 1:
            break
        for w in range(2):
            for m in range(5, -1, -1):
                late = [below[m, n] * solved[w][n] for n in range(m // 2 * 2 + 2, 8)]
                solved[w][m] = solved[w][m] - tree(late)
        next_l, next_r = [], []
        for q in range(1, groups - p):
            raw = [jnp.broadcast_to(left[q][:, 8 * p + m : 8 * p + m + 1], tile) for m in range(8)]
            next_l.append(left[q] - tree([raw[m] * solved[0][m] for m in range(8)]))
            next_r.append(right[q] - tree([raw[m] * solved[1][m] for m in range(8)]))
        left, right = next_l, next_r
    return jnp.concatenate(upper, 0), jnp.concatenate(inverse, 0)


def kernel(
    n_x, n_y, n_z,
    order_ref, columns_ref, rows_ref, bar_ref, inv_ref, border_ref, panel_ref,
    diag_ref, slab_ref,
    order_in, columns_in, rows_in, bar_in, factor_in, border_in,
    pb, tr, coup, coup_in, packed, c_buf, half, z_buf, z_sum, l_buf, y_own, y_buf,
    x_own, x_buf, full, maps, flat_buf, row_map, wide, total, pc_buf, p_half, pz_buf,
    work, upper, inverse, turned,
    send_sem, recv_sem, local_sem,
):
    scen, col = lax.axis_index("scen"), lax.axis_index("col")
    core, l, z = scen % 2, (scen // 2) % 2, scen // 4
    x, y = col // n_y, col % n_y
    zy, n_zy = scen // 2, 2 * n_z
    sibling = scen + 1 - 2 * core
    beside_y = scen + 2 - 4 * l
    first, rest = 16 // n_z, 24 // n_z
    parts = (pl.ds(0, first), pl.ds(first, rest))
    p_rows = total.shape[0] // 2
    p_chunk = p_rows // n_zy
    p_size = inv_ref.shape[1]
    n_scen, n_b = rows_ref.shape[1:]
    wire = Wire(send_sem, recv_sem)

    with jax.named_scope("barrier"):
        loads = [
            pltpu.make_async_copy(src, dst, local_sem.at[k])
            for k, (src, dst) in enumerate(
                (
                    (inv_ref.at[0], factor_in),
                    (border_ref.at[0], border_in),
                    (order_ref, order_in),
                    (columns_ref, columns_in),
                    (rows_ref, rows_in),
                    (bar_ref, bar_in),
                    (panel_ref.at[0, pl.ds(x * n_y, n_y)], pb.at[:, x]),
                )
            )
        ]
        for load in loads:
            load.start()
        barrier = pltpu.get_barrier_semaphore()
        zy_peers = [((zy + d) % n_zy) * 2 + core for d in range(1, n_zy)]
        z_peers = [(z + d) % n_z for d in range(1, n_z)]
        y_peers = [(y + d) % n_y for d in range(1, n_y)]
        x_peers = [(x + d) % n_x for d in range(1, n_x)]
        greet = [(sibling, col)] + [(p, col) for p in zy_peers]
        greet += [(scen, x * n_y + p) for p in y_peers] + [(scen, p * n_y + y) for p in x_peers]
        for device in greet:
            pl.semaphore_signal(barrier, inc=1, device_id=device, device_id_type=MESH)

    def arrive(copies):
        for copy in copies:
            copy.wait_recv()

    with jax.named_scope("transform"):
        for load in loads[:4]:
            load.wait()
        order = order_in[0]
        border = border_in[...]
        inside = lax.broadcasted_iota(jnp.int32, border.shape, 1) < order
        cut = jnp.where(inside, border.astype(F32), 0.0).astype(BF16)
        moved = dot(cut, factor_in[...], 1, 0)
        moved = jnp.where(inside, moved, 0.0).astype(BF16)
        tr[y] = moved
        pl.semaphore_wait(barrier, len(greet))
        near = [(y + 1) % n_y] + ([(y + n_y - 1) % n_y] if n_y > 2 else [])
        tr_copies = wire.start(
            [(tr.at[y], tr.at[y], scen, x * n_y + p) for p in near], tr.at[pl.ds(0, len(near))]
        )
        pb_copies = wire.start(
            [(panel_ref.at[0, pl.ds(p * n_y, n_y)], pb.at[:, x], scen, p * n_y + y) for p in x_peers],
            pb.at[:, pl.ds(0, n_x - 1)],
        )

    with jax.named_scope("diag"):
        terms = 0.5 * (dot(border, moved, 1, 1) + dot(moved, border, 1, 1))
        own_map = one_hot(columns_in[pl.ds(col, 1), :], DIAG)
        spread = sum(dot(own_map, piece, 1, 0) for piece in split(terms, 3))
        pieces = split(spread, 3)
        c_copies = []

        def give_core(k):
            return wire.start([(packed.at[1 - core, :, :, parts[k]], c_buf.at[:, :, parts[k]], sibling, col)])

        for r in range(NB):
            rows = slice(128 * r, 128 * r + 128)
            strip = sum(dot(piece[rows], own_map[128 * r :], 1, 1) for piece in pieces)
            for j in range(r, NB):
                block = strip[:, 128 * (j - r) : 128 * (j - r + 1)]
                for t in range(16):
                    packed[where_tile(n_z, r, j, t)] = block[8 * t : 8 * t + 8]
            if r == 0:
                c_copies.append(give_core(0))
        c_copies.append(give_core(1))

    def add_cores(k):
        arrive(c_copies[k])
        half[:, :, parts[k]] = packed[core, :, :, parts[k]] + c_buf[:, :, parts[k]]
        return wire.start(
            [
                (half.at[p, :, parts[k]], z_buf.at[i, :, parts[k]], p * 4 + l * 2 + core, col)
                for i, p in enumerate(z_peers)
            ],
            z_buf.at[:, :, parts[k]],
        )

    def add_z(k, copies):
        arrive(copies)
        mine = half[z, :, parts[k]]
        z_sum[:, parts[k]] = mine + jnp.sum(z_buf[:, :, parts[k]], axis=0) if n_z > 1 else mine
        return wire.start([(z_sum.at[1 - l, parts[k]], l_buf.at[parts[k]], beside_y, col)])

    def add_l(k, copies):
        arrive(copies)
        y_own[parts[k]] = z_sum[l, parts[k]] + l_buf[parts[k]]
        return wire.start(
            [(y_own.at[parts[k]], y_buf.at[i, parts[k]], scen, x * n_y + p) for i, p in enumerate(y_peers)],
            y_buf.at[:, parts[k]],
        )

    def add_y(k, copies):
        arrive(copies)
        x_own[parts[k]] = y_own[parts[k]] + jnp.sum(y_buf[:, parts[k]], axis=0)
        return wire.start(
            [(x_own.at[parts[k]], x_buf.at[i, parts[k]], scen, p * n_y + y) for i, p in enumerate(x_peers)],
            x_buf.at[:, parts[k]],
        )

    def add_x(k, copies):
        arrive(copies)
        full[core, z, l, parts[k]] = x_own[parts[k]] + jnp.sum(x_buf[:, parts[k]], axis=0)
        here = full.at[core, z, l, parts[k]]
        return wire.start([(here, here, beside_y, col)])

    def gather_z(k, copies):
        arrive(copies)
        here = full.at[core, z, :, parts[k]]
        return wire.start(
            [(here, here, p * 4 + l * 2 + core, col) for p in z_peers],
            full.at[0, pl.ds(0, max(n_z - 1, 1)), :, parts[k]],
        )

    def gather_cores(k, copies):
        arrive(copies)
        here = full.at[core, :, :, parts[k]]
        return wire.start([(here, here, sibling, col)])

    def couple(i):
        stacked = pb[i].reshape(n_x * n_b, p_size)
        coup[i] = dot(stacked, tr[i], 1, 1).reshape(coup.shape[1:])
        coup_in[x * n_y + i] = coup[i, x]

    def give(some):
        return wire.start(
            [(coup.at[i, p], coup_in.at[x * n_y + i], scen, p * n_y + y) for i in some for p in x_peers],
            coup.at[pl.ds(0, len(some)), pl.ds(0, n_x - 1)],
        )

    def widen(i):
        high, low = split(coup_in[i], 2)
        both = dot(jnp.concatenate([high, low], axis=0), maps[i], 1, 1)
        at = i * n_b
        wide[pl.ds(pl.multiple_of(at, 16), n_b), :] = both[:n_b] + both[n_b:]

    with jax.named_scope("cores0"):
        s0 = add_cores(0)
    with jax.named_scope("cores1"):
        s1 = add_cores(1)
    with jax.named_scope("maps"):
        loads[4].wait()
        loads[5].wait()
        for i in range(n_scen):
            flat_buf[:, n_b * i : n_b * i + n_b] = rows_in[0, i : i + 1, :]
        flat = flat_buf[...]
        owner = (flat * 4370) >> 16
        slot = (owner % 2) * p_rows + (owner // 2) * p_chunk + (flat - owner * 15)
        row_map[...] = one_hot(slot, 2 * p_rows)

        def build_map(i, carry):
            maps[i] = one_hot(columns_in[pl.ds(i, 1), :], DIAG)
            return carry

        lax.fori_loop(0, n_scen, build_map, 0)
        upper[...] = jnp.zeros(upper.shape, F32)
    with jax.named_scope("z0"):
        s0 = add_z(0, s0)
    far = (y + 2) % n_y
    with jax.named_scope("l0"):
        s0 = add_l(0, s0)
    with jax.named_scope("z1"):
        s1 = add_z(1, s1)
    with jax.named_scope("tr_wait"):
        arrive(tr_copies)
        far_copies = []
        if n_y == 4:
            h = tr.shape[1] // 2
            up, down = (y + 1) % n_y, (y + n_y - 1) % n_y
            low_half, high_half = tr.at[down, pl.ds(0, h)], tr.at[up, pl.ds(h, h)]
            far_copies = wire.start(
                [(low_half, low_half, scen, x * n_y + up), (high_half, high_half, scen, x * n_y + down)], tr.at[0]
            )
        loads[6].wait()
        arrive(pb_copies)
    with jax.named_scope("couple"):
        for i in [y] + near:
            couple(i)
    with jax.named_scope("y0"):
        s0 = add_y(0, s0)
        q_near = give([y] + near)
    with jax.named_scope("l1"):
        s1 = add_l(1, s1)
    with jax.named_scope("x0"):
        s0 = add_x(0, s0)
    with jax.named_scope("lg0"):
        s0 = gather_z(0, s0)
    with jax.named_scope("y1"):
        s1 = add_y(1, s1)
    with jax.named_scope("far"):
        q_far = []
        if n_y == 4:
            arrive(far_copies)
            couple(far)
            q_far = give([far])
    with jax.named_scope("q_near"):
        arrive(q_near)
    with jax.named_scope("widen_near"):
        for i in [y] + near:
            for k in range(n_x):
                widen(k * n_y + i)
    with jax.named_scope("x1"):
        s1 = add_x(1, s1)
    with jax.named_scope("zg0"):
        s0 = gather_cores(0, s0)
    with jax.named_scope("lg1"):
        s1 = gather_z(1, s1)
    with jax.named_scope("q_far"):
        arrive(q_far)
    with jax.named_scope("widen_far"):
        if n_y == 4:
            for k in range(n_x):
                widen(k * n_y + far)
    with jax.named_scope("total"):
        high, low = split(wide[...], 2)
        total[...] = dot(row_map[...], high, 1, 0) + dot(row_map[...], low, 1, 0)
        pc_copies = wire.start([(total.at[pl.ds((1 - core) * p_rows, p_rows)], pc_buf, sibling, col)])
    with jax.named_scope("drain0"):
        wire.drain(4)
    with jax.named_scope("hg0"):
        arrive(s0)

    rr = lax.broadcasted_iota(jnp.int32, (128, 128), 0)
    cc = lax.broadcasted_iota(jnp.int32, (128, 128), 1)

    def load_row(r):
        for j in range(r, NB):
            block = jnp.concatenate([full[where_tile(n_z, r, j, t)] for t in range(16)], axis=0)
            if r == j:
                block = block + jnp.where(rr == cc, bar_in[:, 128 * r : 128 * r + 128], 0.0)
            work[128 * r : 128 * r + 128, 128 * j : 128 * j + 128] = block

    zero = jnp.broadcast_to(bar_in[:, :128] * 0.0, (8, 128))

    def block_step(o):
        with jax.named_scope("block"):
            u, inv = factor_block(work[pl.ds(o, 128), pl.ds(o, 128)], zero)
            upper[pl.ds(o, 128), pl.ds(o, 128)] = u
            inverse[pl.ds(o, 128), :] = inv
        return inv

    def lead_row(k, inv):
        s = 128 * k
        upper[s : s + 128, s + 128 :] = dot(inv, work[s : s + 128, s + 128 :], 1, 0, HIGHEST)

    def trail(k):
        with jax.named_scope("trail"):
            s = 128 * k
            beside = upper[s : s + 128, s + 128 :]
            for j in range(k + 1, NB):
                lead = beside[:, 128 * (j - k - 1) : 128 * (j - k)]
                tail = beside[:, 128 * (j - k - 1) :]
                work[128 * j : 128 * j + 128, 128 * j :] -= dot(lead, tail, 0, 0, HIGHEST)

    load_row(0)
    inv = block_step(0)
    with jax.named_scope("zg1"):
        s1 = gather_cores(1, s1)
    with jax.named_scope("pc_wait"):
        arrive(pc_copies)
        p_half[...] = total[pl.ds(core * p_rows, p_rows)] + pc_buf[...]
        pz_copies = wire.start(
            [
                (p_half.at[pl.ds(((zy + d) % n_zy) * p_chunk, p_chunk)], pz_buf.at[d - 1], zy_peers[d - 1], col)
                for d in range(1, n_zy)
            ],
            pz_buf,
        )
    with jax.named_scope("hg1"):
        lead_row(0, inv)
        arrive(s1)
        for r in range(1, NB):
            load_row(r)
    trail(0)

    def step(b, carry):
        inv = block_step(pl.multiple_of(b * 128, 128))
        for k in range(1, NB - 1):

            @pl.when(b == k)
            def _():
                lead_row(k, inv)
                trail(k)

        return carry

    lax.fori_loop(1, NB, step, 0)

    with jax.named_scope("pick"):
        n_out = diag_ref.shape[0]
        start = col * n_out
        turned[...] = jnp.transpose(upper[:, pl.ds(pl.multiple_of(start // 128 * 128, 128), 128)])
        diag_ref[...] = turned[pl.ds(pl.multiple_of(start % 128, 8), n_out), :]
    with jax.named_scope("pz_wait"):
        arrive(pz_copies)
    with jax.named_scope("solve"):
        rows = p_half[pl.ds(zy * p_chunk, p_chunk)] + jnp.sum(pz_buf[...], axis=0)
        solved = []
        for b in range(NB):
            done = dot(rows[:, :128], inverse[128 * b : 128 * b + 128, :], 1, 1, HIGHEST)
            solved.append(done)
            if b < NB - 1:
                rows = rows[:, 128:] - dot(done, upper[128 * b : 128 * b + 128, 128 * b + 128 :], 1, 0, HIGHEST)
        slab_ref[...] = jnp.concatenate(solved, axis=1)[: slab_ref.shape[0]]
    with jax.named_scope("drain1"):
        wire.drain()


def out_kernel(diag_ref, slab_ref, diag_out, slab_out):
    diag_out[...] = diag_ref[...]
    slab_out[...] = slab_ref[...]


def where_tile(n_z, r, j, t):
    first, rest = 16 // n_z, 24 // n_z
    at = 16 * BLOCKS.index((r, j)) + t
    if r == 0:
        chunk, e = at // first, at % first
    else:
        at -= 16 * NB
        chunk, e = at // rest, first + at % rest
    return chunk // (2 * n_z), chunk // 2 % n_z, chunk % 2, e


def shards(
    inverse_factor, true_orders, slab_border, slab_columns, panel_border, panel_rows, barrier_diag
):
    n_col = lax.axis_size("col")
    n_z = lax.axis_size("scen") // 4
    n_y = min(n_col, 4) if n_col != 4 else 2
    n_x = n_col // n_y
    n_scen = slab_columns.shape[0]
    cbj, p_size = slab_border.shape[1:]
    cbp = panel_border.shape[2]
    chunk = TILES // 4 // n_z
    p_rows = 32 * n_z
    n_copies = 23
    tile = (8, 128)
    vmem = pl.BlockSpec(memory_space=pltpu.VMEM)
    anywhere = pl.BlockSpec(memory_space=pl.ANY)
    scratch = [
        pltpu.SMEM((1,), jnp.int32),
        pltpu.VMEM(slab_columns.shape, jnp.int32),
        pltpu.VMEM(panel_rows.shape, jnp.int32),
        pltpu.VMEM((1, DIAG), F32),
        pltpu.VMEM((p_size, p_size), BF16),
        pltpu.VMEM((cbj, p_size), BF16),
        pltpu.VMEM((n_y, n_x, cbp, p_size), BF16),
        pltpu.VMEM((n_y, cbj, p_size), BF16),
        pltpu.VMEM((n_y, n_x, cbp, cbj), F32),
        pltpu.VMEM((n_scen, cbp, cbj), F32),
        pltpu.VMEM((2, n_z, 2, chunk) + tile, F32),
        pltpu.VMEM((n_z, 2, chunk) + tile, F32),
        pltpu.VMEM((n_z, 2, chunk) + tile, F32),
        pltpu.VMEM((max(n_z - 1, 1), 2, chunk) + tile, F32),
        pltpu.VMEM((2, chunk) + tile, F32),
        pltpu.VMEM((chunk,) + tile, F32),
        pltpu.VMEM((chunk,) + tile, F32),
        pltpu.VMEM((n_y - 1, chunk) + tile, F32),
        pltpu.VMEM((chunk,) + tile, F32),
        pltpu.VMEM((max(n_x - 1, 1), chunk) + tile, F32),
        pltpu.VMEM((2, n_z, 2, chunk) + tile, F32),
        pltpu.VMEM((n_scen, DIAG, cbj), BF16),
        pltpu.VMEM((1, n_scen * cbp), jnp.int32),
        pltpu.VMEM((2 * p_rows, n_scen * cbp), BF16),
        pltpu.VMEM((n_scen * cbp, DIAG), F32),
        pltpu.VMEM((2 * p_rows, DIAG), F32),
        pltpu.VMEM((p_rows, DIAG), F32),
        pltpu.VMEM((p_rows, DIAG), F32),
        pltpu.VMEM((2 * n_z - 1, 16, DIAG), F32),
        pltpu.VMEM((DIAG, DIAG), F32),
        pltpu.VMEM((DIAG, DIAG), F32),
        pltpu.VMEM((DIAG, 128), F32),
        pltpu.VMEM((128, DIAG), F32),
        pltpu.SemaphoreType.DMA((n_copies,)),
        pltpu.SemaphoreType.DMA((n_copies,)),
        pltpu.SemaphoreType.DMA((7,)),
    ]
    factored = pl.pallas_call(
        functools.partial(kernel, n_x, n_y, n_z),
        name="slab",
        out_shape=tuple(
            pltpu.VMEM(shape, F32) for shape in ((DIAG // n_col, DIAG), (15, DIAG))
        ),
        in_specs=[anywhere] * 7,
        out_specs=[vmem] * 2,
        scratch_shapes=scratch,
        compiler_params=pltpu.CompilerParams(collective_id=0, has_side_effects=True),
    )(
        true_orders,
        slab_columns,
        panel_rows,
        barrier_diag.reshape(1, DIAG),
        inverse_factor,
        slab_border,
        panel_border,
    )
    return pl.pallas_call(
        out_kernel,
        name="out",
        out_shape=(
            jax.ShapeDtypeStruct((DIAG // n_col, DIAG), F32),
            jax.ShapeDtypeStruct((15, DIAG), F32),
        ),
        in_specs=[vmem] * 2,
        out_specs=[vmem] * 2,
    )(*(pltpu.with_memory_space_constraint(one, pltpu.VMEM) for one in factored))


def solution(mesh):
    in_specs = (
        P(("scen", "col"), None, None),
        P(("scen", "col")),
        P(("scen", "col"), None, None),
        P("scen", None),
        P("col", "scen", None, None),
        P("col", "scen", None),
        P(),
    )
    out_specs = (P("col", None), P(("scen", "col"), None))
    return jax.shard_map(shards, mesh=mesh, in_specs=in_specs, out_specs=out_specs, check_vma=False)
```

```python
import functools

import jax
import jax.numpy as jnp
from jax import lax
from jax.experimental import pallas as pl
from jax.experimental.pallas import tpu as pltpu
from jax.sharding import PartitionSpec as P

HIGHEST = lax.Precision.HIGHEST
MESH = pl.DeviceIdType.MESH
F32 = jnp.float32
BF16 = jnp.bfloat16
DIAG = 512
NB = DIAG // 128
BLOCKS = [(r, j) for r in range(NB) for j in range(r, NB)]
TILES = 16 * len(BLOCKS)


def split(value, parts):
    out = []
    for _ in range(parts - 1):
        piece = value.astype(BF16)
        out.append(piece)
        value = value - piece.astype(F32)
    return out + [value.astype(BF16)]


def dot(a, b, ca, cb, precision=None):
    return lax.dot_general(
        a, b, (((ca,), (cb,)), ((), ())), precision=precision, preferred_element_type=F32
    )


def one_hot(targets, height):
    width = targets.shape[1]
    place = lax.broadcasted_iota(jnp.int32, (height, width), 0)
    return jnp.where(place == targets, 1.0, 0.0).astype(BF16)


class Wire:
    def __init__(self, send_sem, recv_sem):
        self.send_sem, self.recv_sem, self.used, self.sends = send_sem, recv_sem, 0, []

    def start(self, group, view=None):
        sems = self.send_sem.at[self.used], self.recv_sem.at[self.used]
        self.used += 1
        for src, dst, scen, col in group:
            pltpu.make_async_remote_copy(src, dst, *sems, (scen, col), MESH).start()
        if group:
            view = group[0][1] if view is None else view
            whole = pltpu.make_async_remote_copy(view, view, *sems, group[0][2:], MESH)
            self.sends.append(whole)
            return [whole]
        return []

    def drain(self, keep=0):
        done = len(self.sends) - keep
        for copy in self.sends[:done]:
            copy.wait_send()
        self.sends = self.sends[done:]


def tree(terms):
    while len(terms) > 1:
        terms = [sum(terms[i : i + 2]) for i in range(0, len(terms), 2)]
    return terms[0]


def factor_block(block, zero):
    groups = 16
    tile = (8, 128)
    lane = lax.broadcasted_iota(jnp.int32, tile, 1)
    sub = lax.broadcasted_iota(jnp.int32, tile, 0)
    whole = (groups,) + tile
    left = block.reshape(whole)
    place = 8 * lax.broadcasted_iota(jnp.int32, whole, 0) + lax.broadcasted_iota(jnp.int32, whole, 1)
    right = jnp.where(lax.broadcasted_iota(jnp.int32, whole, 2) == place, 1.0, 0.0)
    upper, inverse = [], []

    def spread(value, m):
        return jnp.broadcast_to(value[m : m + 1], tile)

    for p in range(groups):
        rows = [left[0], right[0]]
        column = [jnp.broadcast_to(rows[0][:, 8 * p + m : 8 * p + m + 1], tile) + zero for m in range(8)]
        out = [jnp.zeros(tile, F32)] * 2
        below, solved = {}, [[None] * 8, [None] * 8]
        for m in range(0, 8, 2):
            k = m + 1
            col_m, col_k = column[m], column[k]
            a, b, c = spread(col_m, m), spread(col_k, m), spread(col_k, k)
            det = a * c - b * b
            over = 1.0 / det
            ia, ib, ic = c * over, -(b * over), a * over
            for n in range(k + 1, 8):
                e, f = spread(column[n], m), spread(column[n], k)
                g, h = ia * e + ib * f, ib * e + ic * f
                below[m, n], below[k, n] = g, h
                column[n] = column[n] - (col_m * g + col_k * h)
            s0 = lax.rsqrt(a)
            s1 = lax.rsqrt(det) * (a * s0)
            ratio = b * s0 * s0
            under = sub > k
            for w in range(2):
                first, second = spread(rows[w], m), spread(rows[w], k)
                y0, y1 = ia * first + ib * second, ib * first + ic * second
                solved[w][m], solved[w][k] = y0, y1
                if k < 7:
                    rows[w] = rows[w] - jnp.where(under, col_m * y0 + col_k * y1, 0.0)
                out[w] = jnp.where(
                    sub == m, first * s0, jnp.where(sub == k, (second - ratio * first) * s1, out[w])
                )
        upper.append(jnp.where(lane >= sub + 8 * p, out[0], 0.0))
        inverse.append(out[1])
        if p == groups - 1:
            break
        for w in range(2):
            for m in range(5, -1, -1):
                late = [below[m, n] * solved[w][n] for n in range(m // 2 * 2 + 2, 8)]
                solved[w][m] = solved[w][m] - tree(late)
        next_l, next_r = [], []
        for q in range(1, groups - p):
            raw = [jnp.broadcast_to(left[q][:, 8 * p + m : 8 * p + m + 1], tile) for m in range(8)]
            next_l.append(left[q] - tree([raw[m] * solved[0][m] for m in range(8)]))
            next_r.append(right[q] - tree([raw[m] * solved[1][m] for m in range(8)]))
        left, right = next_l, next_r
    return jnp.concatenate(upper, 0), jnp.concatenate(inverse, 0)


def kernel(
    n_x, n_y, n_z,
    order_ref, columns_ref, rows_ref, bar_ref, inv_ref, border_ref, panel_ref,
    diag_ref, slab_ref,
    order_in, columns_in, rows_in, bar_in, factor_in, border_in,
    pb, tr, coup, coup_in, packed, c_buf, half, z_buf, z_sum, l_buf, y_own, y_buf,
    x_own, x_buf, full, maps, flat_buf, row_map, wide, total, pc_buf, p_half, pz_buf,
    work, upper, inverse, turned,
    send_sem, recv_sem, local_sem,
):
    scen, col = lax.axis_index("scen"), lax.axis_index("col")
    core, l, z = scen % 2, (scen // 2) % 2, scen // 4
    x, y = col // n_y, col % n_y
    zy, n_zy = scen // 2, 2 * n_z
    sibling = scen + 1 - 2 * core
    beside_y = scen + 2 - 4 * l
    first, rest = 16 // n_z, 24 // n_z
    parts = (pl.ds(0, first), pl.ds(first, rest))
    p_rows = total.shape[0] // 2
    p_chunk = p_rows // n_zy
    p_size = inv_ref.shape[1]
    n_scen, n_b = rows_ref.shape[1:]
    wire = Wire(send_sem, recv_sem)

    with jax.named_scope("barrier"):
        loads = [
            pltpu.make_async_copy(src, dst, local_sem.at[k])
            for k, (src, dst) in enumerate(
                (
                    (inv_ref.at[0], factor_in),
                    (border_ref.at[0], border_in),
                    (order_ref, order_in),
                    (columns_ref, columns_in),
                    (rows_ref, rows_in),
                    (bar_ref, bar_in),
                    (panel_ref.at[0, pl.ds(x * n_y, n_y)], pb.at[:, x]),
                )
            )
        ]
        for load in loads:
            load.start()
        barrier = pltpu.get_barrier_semaphore()
        zy_peers = [((zy + d) % n_zy) * 2 + core for d in range(1, n_zy)]
        z_peers = [(z + d) % n_z for d in range(1, n_z)]
        y_peers = [(y + d) % n_y for d in range(1, n_y)]
        x_peers = [(x + d) % n_x for d in range(1, n_x)]
        greet = [(sibling, col)] + [(p, col) for p in zy_peers]
        greet += [(scen, x * n_y + p) for p in y_peers] + [(scen, p * n_y + y) for p in x_peers]
        for device in greet:
            pl.semaphore_signal(barrier, inc=1, device_id=device, device_id_type=MESH)

    def arrive(copies):
        for copy in copies:
            copy.wait_recv()

    with jax.named_scope("transform"):
        for load in loads[:4]:
            load.wait()
        order = order_in[0]
        border = border_in[...]
        inside = lax.broadcasted_iota(jnp.int32, border.shape, 1) < order
        cut = jnp.where(inside, border.astype(F32), 0.0).astype(BF16)
        moved = dot(cut, factor_in[...], 1, 0)
        moved = jnp.where(inside, moved, 0.0).astype(BF16)
        tr[y] = moved
        pl.semaphore_wait(barrier, len(greet))
        near = [(y + 1) % n_y] + ([(y + n_y - 1) % n_y] if n_y > 2 else [])
        tr_copies = wire.start(
            [(tr.at[y], tr.at[y], scen, x * n_y + p) for p in near], tr.at[pl.ds(0, len(near))]
        )
        pb_copies = wire.start(
            [(panel_ref.at[0, pl.ds(p * n_y, n_y)], pb.at[:, x], scen, p * n_y + y) for p in x_peers],
            pb.at[:, pl.ds(0, n_x - 1)],
        )

    with jax.named_scope("diag"):
        terms = 0.5 * (dot(border, moved, 1, 1) + dot(moved, border, 1, 1))
        own_map = one_hot(columns_in[pl.ds(col, 1), :], DIAG)
        spread = sum(dot(own_map, piece, 1, 0) for piece in split(terms, 3))
        pieces = split(spread, 3)
        c_copies = []

        def give_core(k):
            return wire.start([(packed.at[1 - core, :, :, parts[k]], c_buf.at[:, :, parts[k]], sibling, col)])

        for r in range(NB):
            rows = slice(128 * r, 128 * r + 128)
            strip = sum(dot(piece[rows], own_map[128 * r :], 1, 1) for piece in pieces)
            for j in range(r, NB):
                block = strip[:, 128 * (j - r) : 128 * (j - r + 1)]
                for t in range(16):
                    packed[where_tile(n_z, r, j, t)] = block[8 * t : 8 * t + 8]
            if r == 0:
                c_copies.append(give_core(0))
        c_copies.append(give_core(1))

    def add_cores(k):
        arrive(c_copies[k])
        half[:, :, parts[k]] = packed[core, :, :, parts[k]] + c_buf[:, :, parts[k]]
        return wire.start(
            [
                (half.at[p, :, parts[k]], z_buf.at[i, :, parts[k]], p * 4 + l * 2 + core, col)
                for i, p in enumerate(z_peers)
            ],
            z_buf.at[:, :, parts[k]],
        )

    def add_z(k, copies):
        arrive(copies)
        mine = half[z, :, parts[k]]
        z_sum[:, parts[k]] = mine + jnp.sum(z_buf[:, :, parts[k]], axis=0) if n_z > 1 else mine
        return wire.start([(z_sum.at[1 - l, parts[k]], l_buf.at[parts[k]], beside_y, col)])

    def add_l(k, copies):
        arrive(copies)
        y_own[parts[k]] = z_sum[l, parts[k]] + l_buf[parts[k]]
        return wire.start(
            [(y_own.at[parts[k]], y_buf.at[i, parts[k]], scen, x * n_y + p) for i, p in enumerate(y_peers)],
            y_buf.at[:, parts[k]],
        )

    def add_y(k, copies):
        arrive(copies)
        x_own[parts[k]] = y_own[parts[k]] + jnp.sum(y_buf[:, parts[k]], axis=0)
        return wire.start(
            [(x_own.at[parts[k]], x_buf.at[i, parts[k]], scen, p * n_y + y) for i, p in enumerate(x_peers)],
            x_buf.at[:, parts[k]],
        )

    def add_x(k, copies):
        arrive(copies)
        full[core, z, l, parts[k]] = x_own[parts[k]] + jnp.sum(x_buf[:, parts[k]], axis=0)
        here = full.at[core, z, l, parts[k]]
        return wire.start([(here, here, beside_y, col)])

    def gather_z(k, copies):
        arrive(copies)
        here = full.at[core, z, :, parts[k]]
        return wire.start(
            [(here, here, p * 4 + l * 2 + core, col) for p in z_peers],
            full.at[0, pl.ds(0, max(n_z - 1, 1)), :, parts[k]],
        )

    def gather_cores(k, copies):
        arrive(copies)
        here = full.at[core, :, :, parts[k]]
        return wire.start([(here, here, sibling, col)])

    def couple(i):
        stacked = pb[i].reshape(n_x * n_b, p_size)
        coup[i] = dot(stacked, tr[i], 1, 1).reshape(coup.shape[1:])
        coup_in[x * n_y + i] = coup[i, x]

    def give(some):
        return wire.start(
            [(coup.at[i, p], coup_in.at[x * n_y + i], scen, p * n_y + y) for i in some for p in x_peers],
            coup.at[pl.ds(0, len(some)), pl.ds(0, n_x - 1)],
        )

    def widen(i):
        high, low = split(coup_in[i], 2)
        both = dot(jnp.concatenate([high, low], axis=0), maps[i], 1, 1)
        at = i * n_b
        wide[pl.ds(pl.multiple_of(at, 16), n_b), :] = both[:n_b] + both[n_b:]

    with jax.named_scope("cores0"):
        s0 = add_cores(0)
    with jax.named_scope("cores1"):
        s1 = add_cores(1)
    with jax.named_scope("maps"):
        loads[4].wait()
        loads[5].wait()
        for i in range(n_scen):
            flat_buf[:, n_b * i : n_b * i + n_b] = rows_in[0, i : i + 1, :]
        flat = flat_buf[...]
        owner = (flat * 4370) >> 16
        slot = (owner % 2) * p_rows + (owner // 2) * p_chunk + (flat - owner * 15)
        row_map[...] = one_hot(slot, 2 * p_rows)

        def build_map(i, carry):
            maps[i] = one_hot(columns_in[pl.ds(i, 1), :], DIAG)
            return carry

        lax.fori_loop(0, n_scen, build_map, 0)
        upper[...] = jnp.zeros(upper.shape, F32)
    with jax.named_scope("z0"):
        s0 = add_z(0, s0)
    far = (y + 2) % n_y
    with jax.named_scope("l0"):
        s0 = add_l(0, s0)
    with jax.named_scope("z1"):
        s1 = add_z(1, s1)
    with jax.named_scope("tr_wait"):
        arrive(tr_copies)
        far_copies = []
        if n_y == 4:
            h = tr.shape[1] // 2
            up, down = (y + 1) % n_y, (y + n_y - 1) % n_y
            low_half, high_half = tr.at[down, pl.ds(0, h)], tr.at[up, pl.ds(h, h)]
            far_copies = wire.start(
                [(low_half, low_half, scen, x * n_y + up), (high_half, high_half, scen, x * n_y + down)], tr.at[0]
            )
        loads[6].wait()
        arrive(pb_copies)
    with jax.named_scope("couple"):
        for i in [y] + near:
            couple(i)
    with jax.named_scope("y0"):
        s0 = add_y(0, s0)
        q_near = give([y] + near)
    with jax.named_scope("l1"):
        s1 = add_l(1, s1)
    with jax.named_scope("x0"):
        s0 = add_x(0, s0)
    with jax.named_scope("y1"):
        s1 = add_y(1, s1)
    with jax.named_scope("lg0"):
        s0 = gather_z(0, s0)
    with jax.named_scope("far"):
        q_far = []
        if n_y == 4:
            arrive(far_copies)
            couple(far)
            q_far = give([far])
    with jax.named_scope("x1"):
        s1 = add_x(1, s1)
    with jax.named_scope("q_near"):
        arrive(q_near)
    with jax.named_scope("widen_near"):
        for i in [y] + near:
            for k in range(n_x):
                widen(k * n_y + i)
    with jax.named_scope("lg1"):
        s1 = gather_z(1, s1)
    with jax.named_scope("zg0"):
        s0 = gather_cores(0, s0)
    with jax.named_scope("q_far"):
        arrive(q_far)
    with jax.named_scope("widen_far"):
        if n_y == 4:
            for k in range(n_x):
                widen(k * n_y + far)
    with jax.named_scope("total"):
        high, low = split(wide[...], 2)
        total[...] = dot(row_map[...], high, 1, 0) + dot(row_map[...], low, 1, 0)
        pc_copies = wire.start([(total.at[pl.ds((1 - core) * p_rows, p_rows)], pc_buf, sibling, col)])
    with jax.named_scope("drain0"):
        wire.drain(5)
    with jax.named_scope("hg0"):
        arrive(s0)

    rr = lax.broadcasted_iota(jnp.int32, (128, 128), 0)
    cc = lax.broadcasted_iota(jnp.int32, (128, 128), 1)

    def load_row(r):
        for j in range(r, NB):
            block = jnp.concatenate([full[where_tile(n_z, r, j, t)] for t in range(16)], axis=0)
            if r == j:
                block = block + jnp.where(rr == cc, bar_in[:, 128 * r : 128 * r + 128], 0.0)
            work[128 * r : 128 * r + 128, 128 * j : 128 * j + 128] = block

    zero = jnp.broadcast_to(bar_in[:, :128] * 0.0, (8, 128))

    def block_step(o):
        with jax.named_scope("block"):
            u, inv = factor_block(work[pl.ds(o, 128), pl.ds(o, 128)], zero)
            upper[pl.ds(o, 128), pl.ds(o, 128)] = u
            inverse[pl.ds(o, 128), :] = inv
        return inv

    def lead_row(k, inv):
        s = 128 * k
        upper[s : s + 128, s + 128 :] = dot(inv, work[s : s + 128, s + 128 :], 1, 0, HIGHEST)

    def trail(k):
        with jax.named_scope("trail"):
            s = 128 * k
            beside = upper[s : s + 128, s + 128 :]
            for j in range(k + 1, NB):
                lead = beside[:, 128 * (j - k - 1) : 128 * (j - k)]
                tail = beside[:, 128 * (j - k - 1) :]
                work[128 * j : 128 * j + 128, 128 * j :] -= dot(lead, tail, 0, 0, HIGHEST)

    load_row(0)
    inv = block_step(0)
    with jax.named_scope("zg1"):
        s1 = gather_cores(1, s1)
    with jax.named_scope("pc_wait"):
        arrive(pc_copies)
        p_half[...] = total[pl.ds(core * p_rows, p_rows)] + pc_buf[...]
        pz_copies = wire.start(
            [
                (p_half.at[pl.ds(((zy + d) % n_zy) * p_chunk, p_chunk)], pz_buf.at[d - 1], zy_peers[d - 1], col)
                for d in range(1, n_zy)
            ],
            pz_buf,
        )
    with jax.named_scope("hg1"):
        lead_row(0, inv)
        arrive(s1)
        for r in range(1, NB):
            load_row(r)
    trail(0)

    def step(b, carry):
        inv = block_step(pl.multiple_of(b * 128, 128))
        for k in range(1, NB - 1):

            @pl.when(b == k)
            def _():
                lead_row(k, inv)
                trail(k)

        return carry

    lax.fori_loop(1, NB, step, 0)

    with jax.named_scope("pick"):
        n_out = diag_ref.shape[0]
        start = col * n_out
        turned[...] = jnp.transpose(upper[:, pl.ds(pl.multiple_of(start // 128 * 128, 128), 128)])
        diag_ref[...] = turned[pl.ds(pl.multiple_of(start % 128, 8), n_out), :]
    with jax.named_scope("pz_wait"):
        arrive(pz_copies)
    with jax.named_scope("solve"):
        rows = p_half[pl.ds(zy * p_chunk, p_chunk)] + jnp.sum(pz_buf[...], axis=0)
        solved = []
        for b in range(NB):
            done = dot(rows[:, :128], inverse[128 * b : 128 * b + 128, :], 1, 1, HIGHEST)
            solved.append(done)
            if b < NB - 1:
                rows = rows[:, 128:] - dot(done, upper[128 * b : 128 * b + 128, 128 * b + 128 :], 1, 0, HIGHEST)
        slab_ref[...] = jnp.concatenate(solved, axis=1)[: slab_ref.shape[0]]
    with jax.named_scope("drain1"):
        wire.drain()


def out_kernel(diag_ref, slab_ref, diag_out, slab_out):
    diag_out[...] = diag_ref[...]
    slab_out[...] = slab_ref[...]


def where_tile(n_z, r, j, t):
    first, rest = 16 // n_z, 24 // n_z
    at = 16 * BLOCKS.index((r, j)) + t
    if r == 0:
        chunk, e = at // first, at % first
    else:
        at -= 16 * NB
        chunk, e = at // rest, first + at % rest
    return chunk // (2 * n_z), chunk // 2 % n_z, chunk % 2, e


def shards(
    inverse_factor, true_orders, slab_border, slab_columns, panel_border, panel_rows, barrier_diag
):
    n_col = lax.axis_size("col")
    n_z = lax.axis_size("scen") // 4
    n_y = min(n_col, 4) if n_col != 4 else 2
    n_x = n_col // n_y
    n_scen = slab_columns.shape[0]
    cbj, p_size = slab_border.shape[1:]
    cbp = panel_border.shape[2]
    chunk = TILES // 4 // n_z
    p_rows = 32 * n_z
    n_copies = 23
    tile = (8, 128)
    vmem = pl.BlockSpec(memory_space=pltpu.VMEM)
    anywhere = pl.BlockSpec(memory_space=pl.ANY)
    scratch = [
        pltpu.SMEM((1,), jnp.int32),
        pltpu.VMEM(slab_columns.shape, jnp.int32),
        pltpu.VMEM(panel_rows.shape, jnp.int32),
        pltpu.VMEM((1, DIAG), F32),
        pltpu.VMEM((p_size, p_size), BF16),
        pltpu.VMEM((cbj, p_size), BF16),
        pltpu.VMEM((n_y, n_x, cbp, p_size), BF16),
        pltpu.VMEM((n_y, cbj, p_size), BF16),
        pltpu.VMEM((n_y, n_x, cbp, cbj), F32),
        pltpu.VMEM((n_scen, cbp, cbj), F32),
        pltpu.VMEM((2, n_z, 2, chunk) + tile, F32),
        pltpu.VMEM((n_z, 2, chunk) + tile, F32),
        pltpu.VMEM((n_z, 2, chunk) + tile, F32),
        pltpu.VMEM((max(n_z - 1, 1), 2, chunk) + tile, F32),
        pltpu.VMEM((2, chunk) + tile, F32),
        pltpu.VMEM((chunk,) + tile, F32),
        pltpu.VMEM((chunk,) + tile, F32),
        pltpu.VMEM((n_y - 1, chunk) + tile, F32),
        pltpu.VMEM((chunk,) + tile, F32),
        pltpu.VMEM((max(n_x - 1, 1), chunk) + tile, F32),
        pltpu.VMEM((2, n_z, 2, chunk) + tile, F32),
        pltpu.VMEM((n_scen, DIAG, cbj), BF16),
        pltpu.VMEM((1, n_scen * cbp), jnp.int32),
        pltpu.VMEM((2 * p_rows, n_scen * cbp), BF16),
        pltpu.VMEM((n_scen * cbp, DIAG), F32),
        pltpu.VMEM((2 * p_rows, DIAG), F32),
        pltpu.VMEM((p_rows, DIAG), F32),
        pltpu.VMEM((p_rows, DIAG), F32),
        pltpu.VMEM((2 * n_z - 1, 16, DIAG), F32),
        pltpu.VMEM((DIAG, DIAG), F32),
        pltpu.VMEM((DIAG, DIAG), F32),
        pltpu.VMEM((DIAG, 128), F32),
        pltpu.VMEM((128, DIAG), F32),
        pltpu.SemaphoreType.DMA((n_copies,)),
        pltpu.SemaphoreType.DMA((n_copies,)),
        pltpu.SemaphoreType.DMA((7,)),
    ]
    factored = pl.pallas_call(
        functools.partial(kernel, n_x, n_y, n_z),
        name="slab",
        out_shape=tuple(
            pltpu.VMEM(shape, F32) for shape in ((DIAG // n_col, DIAG), (15, DIAG))
        ),
        in_specs=[anywhere] * 7,
        out_specs=[vmem] * 2,
        scratch_shapes=scratch,
        compiler_params=pltpu.CompilerParams(collective_id=0, has_side_effects=True),
    )(
        true_orders,
        slab_columns,
        panel_rows,
        barrier_diag.reshape(1, DIAG),
        inverse_factor,
        slab_border,
        panel_border,
    )
    return pl.pallas_call(
        out_kernel,
        name="out",
        out_shape=(
            jax.ShapeDtypeStruct((DIAG // n_col, DIAG), F32),
            jax.ShapeDtypeStruct((15, DIAG), F32),
        ),
        in_specs=[vmem] * 2,
        out_specs=[vmem] * 2,
    )(*(pltpu.with_memory_space_constraint(one, pltpu.VMEM) for one in factored))


def solution(mesh):
    in_specs = (
        P(("scen", "col"), None, None),
        P(("scen", "col")),
        P(("scen", "col"), None, None),
        P("scen", None),
        P("col", "scen", None, None),
        P("col", "scen", None),
        P(),
    )
    out_specs = (P("col", None), P(("scen", "col"), None))
    return jax.shard_map(shards, mesh=mesh, in_specs=in_specs, out_specs=out_specs, check_vma=False)
```

```python
import functools

import jax
import jax.numpy as jnp
from jax import lax
from jax.experimental import pallas as pl
from jax.experimental.pallas import tpu as pltpu
from jax.sharding import PartitionSpec as P

HIGHEST = lax.Precision.HIGHEST
MESH = pl.DeviceIdType.MESH
F32 = jnp.float32
BF16 = jnp.bfloat16
DIAG = 512
NB = DIAG // 128
BLOCKS = [(r, j) for r in range(NB) for j in range(r, NB)]
TILES = 16 * len(BLOCKS)


def split(value, parts):
    out = []
    for _ in range(parts - 1):
        piece = value.astype(BF16)
        out.append(piece)
        value = value - piece.astype(F32)
    return out + [value.astype(BF16)]


def dot(a, b, ca, cb, precision=None):
    return lax.dot_general(
        a, b, (((ca,), (cb,)), ((), ())), precision=precision, preferred_element_type=F32
    )


def dot_halves(a, b, ca, cb):
    rows = a.shape[0]
    (a_high, a_low), (b_high, b_low) = split(a, 2), split(b, 2)
    both = dot(jnp.concatenate([a_high, a_low], axis=0), b_high, ca, cb)
    return both[:rows] + (both[rows:] + dot(a_high, b_low, ca, cb))


def one_hot(targets, height):
    width = targets.shape[1]
    place = lax.broadcasted_iota(jnp.int32, (height, width), 0)
    return jnp.where(place == targets, 1.0, 0.0).astype(BF16)


class Wire:
    def __init__(self, send_sem, recv_sem):
        self.send_sem, self.recv_sem, self.used, self.sends = send_sem, recv_sem, 0, []

    def start(self, group, view=None):
        sems = self.send_sem.at[self.used], self.recv_sem.at[self.used]
        self.used += 1
        for src, dst, scen, col in group:
            pltpu.make_async_remote_copy(src, dst, *sems, (scen, col), MESH).start()
        if group:
            view = group[0][1] if view is None else view
            whole = pltpu.make_async_remote_copy(view, view, *sems, group[0][2:], MESH)
            self.sends.append(whole)
            return [whole]
        return []

    def drain(self, keep=0):
        done = len(self.sends) - keep
        for copy in self.sends[:done]:
            copy.wait_send()
        self.sends = self.sends[done:]


def tree(terms):
    while len(terms) > 1:
        terms = [sum(terms[i : i + 2]) for i in range(0, len(terms), 2)]
    return terms[0]


def factor_block(block, zero):
    groups = 16
    tile = (8, 128)
    lane = lax.broadcasted_iota(jnp.int32, tile, 1)
    sub = lax.broadcasted_iota(jnp.int32, tile, 0)
    whole = (groups,) + tile
    left = block.reshape(whole)
    place = 8 * lax.broadcasted_iota(jnp.int32, whole, 0) + lax.broadcasted_iota(jnp.int32, whole, 1)
    right = jnp.where(lax.broadcasted_iota(jnp.int32, whole, 2) == place, 1.0, 0.0)
    upper, inverse = [], []

    def spread(value, m):
        return jnp.broadcast_to(value[m : m + 1], tile)

    for p in range(groups):
        rows = [left[0], right[0]]
        column = [jnp.broadcast_to(rows[0][:, 8 * p + m : 8 * p + m + 1], tile) + zero for m in range(8)]
        out = [jnp.zeros(tile, F32)] * 2
        below, solved = {}, [[None] * 8, [None] * 8]
        for m in range(0, 8, 2):
            k = m + 1
            col_m, col_k = column[m], column[k]
            a, b, c = spread(col_m, m), spread(col_k, m), spread(col_k, k)
            det = a * c - b * b
            over = 1.0 / det
            ia, ib, ic = c * over, -(b * over), a * over
            for n in range(k + 1, 8):
                e, f = spread(column[n], m), spread(column[n], k)
                g, h = ia * e + ib * f, ib * e + ic * f
                below[m, n], below[k, n] = g, h
                column[n] = column[n] - (col_m * g + col_k * h)
            s0 = lax.rsqrt(a)
            s1 = lax.rsqrt(det) * (a * s0)
            ratio = b * s0 * s0
            under = sub > k
            for w in range(2):
                first, second = spread(rows[w], m), spread(rows[w], k)
                y0, y1 = ia * first + ib * second, ib * first + ic * second
                solved[w][m], solved[w][k] = y0, y1
                if k < 7:
                    rows[w] = rows[w] - jnp.where(under, col_m * y0 + col_k * y1, 0.0)
                out[w] = jnp.where(
                    sub == m, first * s0, jnp.where(sub == k, (second - ratio * first) * s1, out[w])
                )
        upper.append(jnp.where(lane >= sub + 8 * p, out[0], 0.0))
        inverse.append(out[1])
        if p == groups - 1:
            break
        for w in range(2):
            for m in range(5, -1, -1):
                late = [below[m, n] * solved[w][n] for n in range(m // 2 * 2 + 2, 8)]
                solved[w][m] = solved[w][m] - tree(late)
        next_l, next_r = [], []
        for q in range(1, groups - p):
            raw = [jnp.broadcast_to(left[q][:, 8 * p + m : 8 * p + m + 1], tile) for m in range(8)]
            next_l.append(left[q] - tree([raw[m] * solved[0][m] for m in range(8)]))
            next_r.append(right[q] - tree([raw[m] * solved[1][m] for m in range(8)]))
        left, right = next_l, next_r
    return jnp.concatenate(upper, 0), jnp.concatenate(inverse, 0)


def kernel(
    n_x, n_y, n_z,
    order_ref, columns_ref, rows_ref, bar_ref, inv_ref, border_ref, panel_ref,
    diag_ref, slab_ref,
    order_in, columns_in, rows_in, bar_in, factor_in, border_in,
    pb, tr, coup, coup_in, packed, c_buf, half, z_buf, z_sum, l_buf, y_own, y_buf,
    x_own, x_buf, full, maps, flat_buf, row_map, wide, total, pc_buf, p_half, pz_buf,
    work, upper, inverse, turned,
    send_sem, recv_sem, local_sem,
):
    scen, col = lax.axis_index("scen"), lax.axis_index("col")
    core, l, z = scen % 2, (scen // 2) % 2, scen // 4
    x, y = col // n_y, col % n_y
    zy, n_zy = scen // 2, 2 * n_z
    sibling = scen + 1 - 2 * core
    beside_y = scen + 2 - 4 * l
    first, rest = 16 // n_z, 24 // n_z
    parts = (pl.ds(0, first), pl.ds(first, rest))
    p_rows = total.shape[0] // 2
    p_chunk = p_rows // n_zy
    p_size = inv_ref.shape[1]
    n_scen, n_b = rows_ref.shape[1:]
    wire = Wire(send_sem, recv_sem)

    with jax.named_scope("barrier"):
        loads = [
            pltpu.make_async_copy(src, dst, local_sem.at[k])
            for k, (src, dst) in enumerate(
                (
                    (inv_ref.at[0], factor_in),
                    (border_ref.at[0], border_in),
                    (order_ref, order_in),
                    (columns_ref, columns_in),
                    (rows_ref, rows_in),
                    (bar_ref, bar_in),
                    (panel_ref.at[0, pl.ds(x * n_y, n_y)], pb.at[:, x]),
                )
            )
        ]
        for load in loads:
            load.start()
        barrier = pltpu.get_barrier_semaphore()
        zy_peers = [((zy + d) % n_zy) * 2 + core for d in range(1, n_zy)]
        z_peers = [(z + d) % n_z for d in range(1, n_z)]
        y_peers = [(y + d) % n_y for d in range(1, n_y)]
        x_peers = [(x + d) % n_x for d in range(1, n_x)]
        greet = [(sibling, col)] + [(p, col) for p in zy_peers]
        greet += [(scen, x * n_y + p) for p in y_peers] + [(scen, p * n_y + y) for p in x_peers]
        for device in greet:
            pl.semaphore_signal(barrier, inc=1, device_id=device, device_id_type=MESH)

    def arrive(copies):
        for copy in copies:
            copy.wait_recv()

    with jax.named_scope("transform"):
        for load in loads[:4]:
            load.wait()
        order = order_in[0]
        border = border_in[...]
        inside = lax.broadcasted_iota(jnp.int32, border.shape, 1) < order
        cut = jnp.where(inside, border.astype(F32), 0.0).astype(BF16)
        moved = dot(cut, factor_in[...], 1, 0)
        moved = jnp.where(inside, moved, 0.0).astype(BF16)
        tr[y] = moved
        pl.semaphore_wait(barrier, len(greet))
        near = [(y + 1) % n_y] + ([(y + n_y - 1) % n_y] if n_y > 2 else [])
        tr_copies = wire.start(
            [(tr.at[y], tr.at[y], scen, x * n_y + p) for p in near], tr.at[pl.ds(0, len(near))]
        )
        pb_copies = wire.start(
            [(panel_ref.at[0, pl.ds(p * n_y, n_y)], pb.at[:, x], scen, p * n_y + y) for p in x_peers],
            pb.at[:, pl.ds(0, n_x - 1)],
        )

    with jax.named_scope("diag"):
        terms = 0.5 * (dot(border, moved, 1, 1) + dot(moved, border, 1, 1))
        own_map = one_hot(columns_in[pl.ds(col, 1), :], DIAG)
        spread = sum(dot(own_map, piece, 1, 0) for piece in split(terms, 3))
        pieces = split(spread, 3)
        c_copies = []

        def give_core(k):
            return wire.start([(packed.at[1 - core, :, :, parts[k]], c_buf.at[:, :, parts[k]], sibling, col)])

        for r in range(NB):
            rows = slice(128 * r, 128 * r + 128)
            strip = sum(dot(piece[rows], own_map[128 * r :], 1, 1) for piece in pieces)
            for j in range(r, NB):
                block = strip[:, 128 * (j - r) : 128 * (j - r + 1)]
                for t in range(16):
                    packed[where_tile(n_z, r, j, t)] = block[8 * t : 8 * t + 8]
            if r == 0:
                c_copies.append(give_core(0))
        c_copies.append(give_core(1))

    def add_cores(k):
        arrive(c_copies[k])
        half[:, :, parts[k]] = packed[core, :, :, parts[k]] + c_buf[:, :, parts[k]]
        return wire.start(
            [
                (half.at[p, :, parts[k]], z_buf.at[i, :, parts[k]], p * 4 + l * 2 + core, col)
                for i, p in enumerate(z_peers)
            ],
            z_buf.at[:, :, parts[k]],
        )

    def add_z(k, copies):
        arrive(copies)
        mine = half[z, :, parts[k]]
        z_sum[:, parts[k]] = mine + jnp.sum(z_buf[:, :, parts[k]], axis=0) if n_z > 1 else mine
        return wire.start([(z_sum.at[1 - l, parts[k]], l_buf.at[parts[k]], beside_y, col)])

    def add_l(k, copies):
        arrive(copies)
        y_own[parts[k]] = z_sum[l, parts[k]] + l_buf[parts[k]]
        return wire.start(
            [(y_own.at[parts[k]], y_buf.at[i, parts[k]], scen, x * n_y + p) for i, p in enumerate(y_peers)],
            y_buf.at[:, parts[k]],
        )

    def add_y(k, copies):
        arrive(copies)
        x_own[parts[k]] = y_own[parts[k]] + jnp.sum(y_buf[:, parts[k]], axis=0)
        return wire.start(
            [(x_own.at[parts[k]], x_buf.at[i, parts[k]], scen, p * n_y + y) for i, p in enumerate(x_peers)],
            x_buf.at[:, parts[k]],
        )

    def add_x(k, copies):
        arrive(copies)
        full[core, z, l, parts[k]] = x_own[parts[k]] + jnp.sum(x_buf[:, parts[k]], axis=0)
        here = full.at[core, z, l, parts[k]]
        return wire.start([(here, here, beside_y, col)])

    def gather_z(k, copies):
        arrive(copies)
        here = full.at[core, z, :, parts[k]]
        return wire.start(
            [(here, here, p * 4 + l * 2 + core, col) for p in z_peers],
            full.at[0, pl.ds(0, max(n_z - 1, 1)), :, parts[k]],
        )

    def gather_cores(k, copies):
        arrive(copies)
        here = full.at[core, :, :, parts[k]]
        return wire.start([(here, here, sibling, col)])

    def couple(i):
        stacked = pb[i].reshape(n_x * n_b, p_size)
        coup[i] = dot(stacked, tr[i], 1, 1).reshape(coup.shape[1:])
        coup_in[x * n_y + i] = coup[i, x]

    def give(some):
        return wire.start(
            [(coup.at[i, p], coup_in.at[x * n_y + i], scen, p * n_y + y) for i in some for p in x_peers],
            coup.at[pl.ds(0, len(some)), pl.ds(0, n_x - 1)],
        )

    def widen(i):
        high, low = split(coup_in[i], 2)
        both = dot(jnp.concatenate([high, low], axis=0), maps[i], 1, 1)
        at = i * n_b
        wide[pl.ds(pl.multiple_of(at, 16), n_b), :] = both[:n_b] + both[n_b:]

    with jax.named_scope("cores0"):
        s0 = add_cores(0)
    with jax.named_scope("cores1"):
        s1 = add_cores(1)
    with jax.named_scope("maps"):
        loads[4].wait()
        loads[5].wait()
        for i in range(n_scen):
            flat_buf[:, n_b * i : n_b * i + n_b] = rows_in[0, i : i + 1, :]
        flat = flat_buf[...]
        owner = (flat * 4370) >> 16
        slot = (owner % 2) * p_rows + (owner // 2) * p_chunk + (flat - owner * 15)
        row_map[...] = one_hot(slot, 2 * p_rows)

        def build_map(i, carry):
            maps[i] = one_hot(columns_in[pl.ds(i, 1), :], DIAG)
            return carry

        lax.fori_loop(0, n_scen, build_map, 0)
        upper[...] = jnp.zeros(upper.shape, F32)
    with jax.named_scope("z0"):
        s0 = add_z(0, s0)
    far = (y + 2) % n_y
    with jax.named_scope("l0"):
        s0 = add_l(0, s0)
    with jax.named_scope("z1"):
        s1 = add_z(1, s1)
    with jax.named_scope("tr_wait"):
        arrive(tr_copies)
        far_copies = []
        if n_y == 4:
            h = tr.shape[1] // 2
            up, down = (y + 1) % n_y, (y + n_y - 1) % n_y
            low_half, high_half = tr.at[down, pl.ds(0, h)], tr.at[up, pl.ds(h, h)]
            far_copies = wire.start(
                [(low_half, low_half, scen, x * n_y + up), (high_half, high_half, scen, x * n_y + down)], tr.at[0]
            )
        loads[6].wait()
        arrive(pb_copies)
    with jax.named_scope("couple"):
        for i in [y] + near:
            couple(i)
    with jax.named_scope("y0"):
        s0 = add_y(0, s0)
        q_near = give([y] + near)
    with jax.named_scope("l1"):
        s1 = add_l(1, s1)
    with jax.named_scope("x0"):
        s0 = add_x(0, s0)
    with jax.named_scope("y1"):
        s1 = add_y(1, s1)
    with jax.named_scope("lg0"):
        s0 = gather_z(0, s0)
    with jax.named_scope("far"):
        q_far = []
        if n_y == 4:
            arrive(far_copies)
            couple(far)
            q_far = give([far])
    with jax.named_scope("x1"):
        s1 = add_x(1, s1)
    with jax.named_scope("q_near"):
        arrive(q_near)
    with jax.named_scope("widen_near"):
        for i in [y] + near:
            for k in range(n_x):
                widen(k * n_y + i)
    with jax.named_scope("lg1"):
        s1 = gather_z(1, s1)
    with jax.named_scope("zg0"):
        s0 = gather_cores(0, s0)
    with jax.named_scope("q_far"):
        arrive(q_far)
    with jax.named_scope("widen_far"):
        if n_y == 4:
            for k in range(n_x):
                widen(k * n_y + far)
    with jax.named_scope("total"):
        high, low = split(wide[...], 2)
        total[...] = dot(row_map[...], high, 1, 0) + dot(row_map[...], low, 1, 0)
        pc_copies = wire.start([(total.at[pl.ds((1 - core) * p_rows, p_rows)], pc_buf, sibling, col)])
    with jax.named_scope("drain0"):
        wire.drain(5)
    with jax.named_scope("hg0"):
        arrive(s0)

    rr = lax.broadcasted_iota(jnp.int32, (128, 128), 0)
    cc = lax.broadcasted_iota(jnp.int32, (128, 128), 1)

    def load_row(r):
        for j in range(r, NB):
            block = jnp.concatenate([full[where_tile(n_z, r, j, t)] for t in range(16)], axis=0)
            if r == j:
                block = block + jnp.where(rr == cc, bar_in[:, 128 * r : 128 * r + 128], 0.0)
            work[128 * r : 128 * r + 128, 128 * j : 128 * j + 128] = block

    zero = jnp.broadcast_to(bar_in[:, :128] * 0.0, (8, 128))

    def block_step(o):
        with jax.named_scope("block"):
            u, inv = factor_block(work[pl.ds(o, 128), pl.ds(o, 128)], zero)
            upper[pl.ds(o, 128), pl.ds(o, 128)] = u
            inverse[pl.ds(o, 128), :] = inv
        return inv

    def lead_row(k, inv):
        s = 128 * k
        upper[s : s + 128, s + 128 :] = dot(inv, work[s : s + 128, s + 128 :], 1, 0, HIGHEST)

    def trail(k):
        with jax.named_scope("trail"):
            s = 128 * k
            beside = upper[s : s + 128, s + 128 :]
            for j in range(k + 1, NB):
                lead = beside[:, 128 * (j - k - 1) : 128 * (j - k)]
                tail = beside[:, 128 * (j - k - 1) :]
                work[128 * j : 128 * j + 128, 128 * j :] -= dot(lead, tail, 0, 0, HIGHEST)

    load_row(0)
    inv = block_step(0)
    with jax.named_scope("zg1"):
        s1 = gather_cores(1, s1)
    with jax.named_scope("pc_wait"):
        arrive(pc_copies)
        p_half[...] = total[pl.ds(core * p_rows, p_rows)] + pc_buf[...]
        pz_copies = wire.start(
            [
                (p_half.at[pl.ds(((zy + d) % n_zy) * p_chunk, p_chunk)], pz_buf.at[d - 1], zy_peers[d - 1], col)
                for d in range(1, n_zy)
            ],
            pz_buf,
        )
    with jax.named_scope("hg1"):
        lead_row(0, inv)
        arrive(s1)
        for r in range(1, NB):
            load_row(r)
    trail(0)

    def step(b, carry):
        inv = block_step(pl.multiple_of(b * 128, 128))
        for k in range(1, NB - 1):

            @pl.when(b == k)
            def _():
                lead_row(k, inv)
                trail(k)

        return carry

    lax.fori_loop(1, NB, step, 0)

    with jax.named_scope("pick"):
        n_out = diag_ref.shape[0]
        start = col * n_out
        turned[...] = jnp.transpose(upper[:, pl.ds(pl.multiple_of(start // 128 * 128, 128), 128)])
        diag_ref[...] = turned[pl.ds(pl.multiple_of(start % 128, 8), n_out), :]
    with jax.named_scope("pz_wait"):
        arrive(pz_copies)
    with jax.named_scope("solve"):
        rows = p_half[pl.ds(zy * p_chunk, p_chunk)] + jnp.sum(pz_buf[...], axis=0)
        solved = []
        for b in range(NB):
            done = dot_halves(rows[:, :128], inverse[128 * b : 128 * b + 128, :], 1, 1)
            solved.append(done)
            if b < NB - 1:
                rows = rows[:, 128:] - dot_halves(done, upper[128 * b : 128 * b + 128, 128 * b + 128 :], 1, 0)
        slab_ref[...] = jnp.concatenate(solved, axis=1)[: slab_ref.shape[0]]
    with jax.named_scope("drain1"):
        wire.drain()


def out_kernel(diag_ref, slab_ref, diag_out, slab_out):
    diag_out[...] = diag_ref[...]
    slab_out[...] = slab_ref[...]


def where_tile(n_z, r, j, t):
    first, rest = 16 // n_z, 24 // n_z
    at = 16 * BLOCKS.index((r, j)) + t
    if r == 0:
        chunk, e = at // first, at % first
    else:
        at -= 16 * NB
        chunk, e = at // rest, first + at % rest
    return chunk // (2 * n_z), chunk // 2 % n_z, chunk % 2, e


def shards(
    inverse_factor, true_orders, slab_border, slab_columns, panel_border, panel_rows, barrier_diag
):
    n_col = lax.axis_size("col")
    n_z = lax.axis_size("scen") // 4
    n_y = min(n_col, 4) if n_col != 4 else 2
    n_x = n_col // n_y
    n_scen = slab_columns.shape[0]
    cbj, p_size = slab_border.shape[1:]
    cbp = panel_border.shape[2]
    chunk = TILES // 4 // n_z
    p_rows = 32 * n_z
    n_copies = 23
    tile = (8, 128)
    vmem = pl.BlockSpec(memory_space=pltpu.VMEM)
    scratch = [
        pltpu.SMEM((1,), jnp.int32),
        pltpu.VMEM(slab_columns.shape, jnp.int32),
        pltpu.VMEM(panel_rows.shape, jnp.int32),
        pltpu.VMEM((1, DIAG), F32),
        pltpu.VMEM((p_size, p_size), BF16),
        pltpu.VMEM((cbj, p_size), BF16),
        pltpu.VMEM((n_y, n_x, cbp, p_size), BF16),
        pltpu.VMEM((n_y, cbj, p_size), BF16),
        pltpu.VMEM((n_y, n_x, cbp, cbj), F32),
        pltpu.VMEM((n_scen, cbp, cbj), F32),
        pltpu.VMEM((2, n_z, 2, chunk) + tile, F32),
        pltpu.VMEM((n_z, 2, chunk) + tile, F32),
        pltpu.VMEM((n_z, 2, chunk) + tile, F32),
        pltpu.VMEM((max(n_z - 1, 1), 2, chunk) + tile, F32),
        pltpu.VMEM((2, chunk) + tile, F32),
        pltpu.VMEM((chunk,) + tile, F32),
        pltpu.VMEM((chunk,) + tile, F32),
        pltpu.VMEM((n_y - 1, chunk) + tile, F32),
        pltpu.VMEM((chunk,) + tile, F32),
        pltpu.VMEM((max(n_x - 1, 1), chunk) + tile, F32),
        pltpu.VMEM((2, n_z, 2, chunk) + tile, F32),
        pltpu.VMEM((n_scen, DIAG, cbj), BF16),
        pltpu.VMEM((1, n_scen * cbp), jnp.int32),
        pltpu.VMEM((2 * p_rows, n_scen * cbp), BF16),
        pltpu.VMEM((n_scen * cbp, DIAG), F32),
        pltpu.VMEM((2 * p_rows, DIAG), F32),
        pltpu.VMEM((p_rows, DIAG), F32),
        pltpu.VMEM((p_rows, DIAG), F32),
        pltpu.VMEM((2 * n_z - 1, 16, DIAG), F32),
        pltpu.VMEM((DIAG, DIAG), F32),
        pltpu.VMEM((DIAG, DIAG), F32),
        pltpu.VMEM((DIAG, 128), F32),
        pltpu.VMEM((128, DIAG), F32),
        pltpu.SemaphoreType.DMA((n_copies,)),
        pltpu.SemaphoreType.DMA((n_copies,)),
        pltpu.SemaphoreType.DMA((7,)),
    ]
    factored = pl.pallas_call(
        functools.partial(kernel, n_x, n_y, n_z),
        name="slab",
        out_shape=tuple(
            pltpu.VMEM(shape, F32) for shape in ((DIAG // n_col, DIAG), (15, DIAG))
        ),
        in_specs=[pl.BlockSpec(memory_space=pltpu.HBM)] * 7,
        out_specs=[vmem] * 2,
        scratch_shapes=scratch,
        compiler_params=pltpu.CompilerParams(collective_id=0, has_side_effects=True),
    )(
        true_orders,
        slab_columns,
        panel_rows,
        barrier_diag.reshape(1, DIAG),
        inverse_factor,
        slab_border,
        panel_border,
    )
    return pl.pallas_call(
        out_kernel,
        name="out",
        out_shape=(
            jax.ShapeDtypeStruct((DIAG // n_col, DIAG), F32),
            jax.ShapeDtypeStruct((15, DIAG), F32),
        ),
        in_specs=[vmem] * 2,
        out_specs=[vmem] * 2,
    )(*(pltpu.with_memory_space_constraint(one, pltpu.VMEM) for one in factored))


def solution(mesh):
    in_specs = (
        P(("scen", "col"), None, None),
        P(("scen", "col")),
        P(("scen", "col"), None, None),
        P("scen", None),
        P("col", "scen", None, None),
        P("col", "scen", None),
        P(),
    )
    out_specs = (P("col", None), P(("scen", "col"), None))
    return jax.shard_map(shards, mesh=mesh, in_specs=in_specs, out_specs=out_specs, check_vma=False)
```
